512 devices in a mesh: blk: 32 (over y_hi, x, core), chan: 16 (over z, y_lo).
Axes of the slice: x: 4, y: 8 (y_hi: 4, y_lo: 2; y = y_hi * 2 + y_lo), z: 8, core: 2. Of those that a mesh axis runs over, the one named last changes fastest.
Arguments:
- pair_repr: bfloat16 [2048, 2048, 128], P('blk', 'chan'), may hold values from -6 to 6
- chain_lengths: int32 [8], replicated, may hold values from 192 to 256
- norm_gain: float32 [128], replicated, may hold values from 0.1 to 1.9
- norm_bias: float32 [128], replicated, may hold values from -3 to 3
- left_gate: bfloat16 [128, 128], replicated, may hold values from -0.5 to 0.5
- left_value: bfloat16 [128, 128], replicated, may hold values from -0.5 to 0.5
- right_gate: bfloat16 [128, 128], replicated, may hold values from -0.5 to 0.5
- right_value: bfloat16 [128, 128], replicated, may hold values from -0.5 to 0.5
- out_gain: float32 [128], replicated, may hold values from 0.1 to 1.9
- out_bias: float32 [128], replicated, may hold values from -3 to 3
- out_weight: bfloat16 [128, 128], replicated, may hold values from -0.5 to 0.5
- gate_weight: bfloat16 [128, 128], replicated, may hold values from -0.5 to 0.5
Outputs:
- pair_update: bfloat16 [2048, 416, 128], P('blk', 'chan')
The draws below stay inside these ranges and needn't reach their ends.
Inputs may be any that keep to these rules, and one draw needn't show every extreme that they name: Chain slot s covers residues s * 256 to (s + 1) * 256 - 1, of which the first chain_lengths[s] are real and the rest padding.
All inputs are finite; a program needn't handle non-finite values.
Results may differ from the reference program's by a relative error of at most 0.0058.
Values may be sent and summed in bfloat16 or wider, within the bound.
No kernel may reach another device: no remote copies, remote signals or barrier semaphores. Data moves between devices by JAX's collectives and lax.ppermute only.
A program may use at most 64 MiB of HBM per device.

```python
import jax
import jax.numpy as jnp
from jax import lax

C = 128
CH = 128
ROWS_DEV = 64
JD = 13
NCHAIN = 8
NRES = 2048
SLOT = 256
J = 416
N_BLK = 32


def place_ends(result, rng, smallest, largest):
    longest = result.shape.index(max(result.shape))
    spots = []
    for shift in (0, 1):
        where = [jax.random.randint(jax.random.fold_in(rng, axis), (), 0, length) for axis, length in enumerate(result.shape)]
        where[longest] = (where[longest] + shift) % result.shape[longest]
        spots.append(tuple(where))
    return result.at[spots[0]].set(smallest).at[spots[1]].set(largest)


def levels(key, shape, pieces, smallest, high):
    gain, own = 1.0, jax.random.fold_in(key, 6)
    for dim, shards_of in pieces:
        draws = jnp.exp(jax.random.uniform(jax.random.fold_in(own, dim), (shards_of,), jnp.float32, smallest / len(pieces), high / len(pieces)))
        gain = gain * jnp.repeat(draws, shape[dim] // shards_of).reshape([-1 if axis == dim else 1 for axis in range(len(shape))])
    return gain


def bell_draw(own_key, extent, scale, limit, split=(), held_as=jnp.bfloat16):
    result = scale * jax.random.normal(own_key, extent, jnp.float32)
    if split:
        result = result * levels(own_key, extent, split, -0.22, 0.18)
    return jnp.clip(result, -limit, limit).astype(held_as)


def setup_inputs(seed: int = 0) -> dict:
    arg_keys = jax.random.split(jax.random.key(seed), 13)
    pair_repr = bell_draw(arg_keys[0], (NRES, NRES, C), 1.0, 6.0, ((0, 32), (1, 16)))
    chain_lengths = place_ends(jax.random.randint(arg_keys[1], (NCHAIN,), 3 * SLOT // 4, SLOT + 1), jax.random.fold_in(arg_keys[1], 1), 3 * SLOT // 4, SLOT).astype(jnp.int32)
    norm_gain = jnp.clip(1.0 + 0.18 * jax.random.normal(arg_keys[2], (C,), jnp.float32), 0.1, 1.9)
    norm_bias = bell_draw(arg_keys[3], (C,), 0.5, 3.0, (), jnp.float32)
    left_gate = bell_draw(arg_keys[4], (C, CH), C ** -0.5, 0.5)
    left_value = bell_draw(arg_keys[5], (C, CH), C ** -0.5, 0.5)
    right_gate = bell_draw(arg_keys[6], (C, CH), C ** -0.5, 0.5)
    right_value = bell_draw(arg_keys[7], (C, CH), C ** -0.5, 0.5)
    out_gain = jnp.clip(1.0 + 0.18 * jax.random.normal(arg_keys[8], (CH,), jnp.float32), 0.1, 1.9)
    out_bias = bell_draw(arg_keys[9], (CH,), 0.5, 3.0, (), jnp.float32)
    out_weight = bell_draw(arg_keys[10], (CH, C), CH ** -0.5, 0.5)
    gate_weight = bell_draw(arg_keys[11], (C, C), C ** -0.5, 0.5)
    return dict(pair_repr=pair_repr, chain_lengths=chain_lengths, norm_gain=norm_gain, norm_bias=norm_bias, left_gate=left_gate, left_value=left_value, right_gate=right_gate, right_value=right_value, out_gain=out_gain, out_bias=out_bias, out_weight=out_weight, gate_weight=gate_weight)


epsilon = 1e-05

def normalize(values, gain_vec, bias_vec):
    centre = lax.optimization_barrier(jnp.mean(values, axis=-1, keepdims=True))
    centred = values - centre
    spread_sq = lax.optimization_barrier(jnp.mean(centred * centred, axis=-1, keepdims=True))
    return centred * lax.rsqrt(spread_sq + epsilon) * gain_vec + bias_vec

def residue_mask(position, lengths, slot_size):
    chain_id = position // slot_size
    chain_table = jnp.arange(lengths.shape[0], dtype=jnp.int32)
    chain_len = lax.optimization_barrier(jnp.sum(jnp.where(chain_id[:, None] == chain_table[None, :], lengths[None, :], 0), axis=1))
    return (position % slot_size < chain_len).astype(jnp.float32)

def reference(pair_repr, chain_lengths, norm_gain, norm_bias, left_gate, left_value, right_gate, right_value, out_gain, out_bias, out_weight, gate_weight):
    position = jnp.arange(NRES, dtype=jnp.int32)
    residue = residue_mask(position, chain_lengths, SLOT)
    window = (jnp.arange(N_BLK, dtype=jnp.int32)[:, None] * ROWS_DEV + jnp.arange(JD, dtype=jnp.int32)[None, :]).reshape(-1)
    window_normed = normalize(pair_repr[window].astype(jnp.float32), norm_gain, norm_bias).astype(jnp.bfloat16)
    window_flat = window_normed.reshape(-1, C)
    right_mix = jax.nn.sigmoid(jnp.dot(window_flat, right_gate, preferred_element_type=jnp.float32)) * jnp.dot(window_flat, right_value, preferred_element_type=jnp.float32)
    right_mix = right_mix.reshape(J, NRES, CH) * residue[window][:, None, None] * residue[None, :, None]
    right_wide = jnp.transpose(right_mix.astype(jnp.bfloat16).astype(jnp.float32), (2, 0, 1))

    def row_block(block_id):
        start_row = block_id * ROWS_DEV
        block_pair = lax.dynamic_slice_in_dim(pair_repr, start_row, ROWS_DEV, 0)
        normed = normalize(block_pair.astype(jnp.float32), norm_gain, norm_bias).astype(jnp.bfloat16)
        flat_rows = normed.reshape(-1, C)
        left_mix = jax.nn.sigmoid(jnp.dot(flat_rows, left_gate, preferred_element_type=jnp.float32)) * jnp.dot(flat_rows, left_value, preferred_element_type=jnp.float32)
        row_real = lax.dynamic_slice_in_dim(residue, start_row, ROWS_DEV, 0)
        left_mix = left_mix.reshape(ROWS_DEV, NRES, CH) * row_real[:, None, None] * residue[None, :, None]
        left_wide = jnp.transpose(left_mix.astype(jnp.bfloat16).astype(jnp.float32), (2, 0, 1))
        product = jnp.einsum('cik,cjk->cij', left_wide, right_wide).astype(jnp.bfloat16).astype(jnp.float32)
        centre = lax.optimization_barrier(jnp.mean(product, axis=0, keepdims=True))
        centred = product - centre
        spread_sq = lax.optimization_barrier(jnp.mean(centred * centred, axis=0, keepdims=True))
        normed_product = (centred * lax.rsqrt(spread_sq + epsilon) * out_gain[:, None, None] + out_bias[:, None, None]).astype(jnp.bfloat16)
        update = jnp.einsum('cij,cd->ijd', normed_product.astype(jnp.float32), out_weight.astype(jnp.float32))
        gate_rows = normed[:, window]
        gate_value = jax.nn.sigmoid(jnp.einsum('ijd,de->ije', gate_rows.astype(jnp.float32), gate_weight.astype(jnp.float32)))
        return (gate_value * update).astype(jnp.bfloat16)
    blocks_out = lax.map(row_block, jnp.arange(N_BLK, dtype=jnp.int32))
    return blocks_out.reshape(NRES, J, C)
```

```python
import functools

import jax
import jax.numpy as jnp
from jax import lax
from jax.experimental import pallas as pl
from jax.experimental.pallas import tpu as pltpu
from jax.sharding import Mesh
from jax.sharding import PartitionSpec as P

JD = 13
PAD = 16
AXES = (("yh", 4), ("x", 4), ("core", 2), ("z", 8), ("yl", 2))
SPREAD = ("x", "core", "z", "yl")

epsilon = 1e-05

dot = functools.partial(lax.dot_general, preferred_element_type=jnp.float32)


def normalize(values, gain_vec, bias_vec):
    centre = jnp.mean(values, axis=-1, keepdims=True)
    centred = values - centre
    spread_sq = jnp.mean(centred * centred, axis=-1, keepdims=True)
    return centred * lax.rsqrt(spread_sq + epsilon) * gain_vec + bias_vec


def place():
    blk = (lax.axis_index("yh") * 4 + lax.axis_index("x")) * 2 + lax.axis_index("core")
    chan = lax.axis_index("z") * 2 + lax.axis_index("yl")
    return blk, chan


def real_left(lengths, start, slot_size):
    return lengths[start // slot_size] - start % slot_size


def project_kernel(
    limit, slot_size, where, lengths, pair, gain, bias, gate_w, value_w, out, stack, planes
):
    rows, cols, _ = pair.shape
    hidden = gate_w.shape[1]
    step = pl.program_id(0)
    blk, chan = where()

    @pl.when(step == 0)
    def _():
        stack[:hidden] = (gate_w[...].astype(jnp.float32) * 0.5).T.astype(jnp.bfloat16)
        stack[hidden:] = value_w[...].astype(jnp.float32).T.astype(jnp.bfloat16)

    row_count = real_left(lengths, blk * limit, slot_size) - step * rows
    col_count = real_left(lengths, chan * cols, slot_size)
    col_ids = lax.broadcasted_iota(jnp.int32, (1, cols), 1)

    def body(i, carry):
        normed = normalize(pair[i].astype(jnp.float32), gain[...], bias[...])
        mix = dot(stack[...], normed.astype(jnp.bfloat16), (((1,), (1,)), ((), ())))
        kept = jnp.where(i < row_count, col_count, 0)
        mask = jnp.where(col_ids < kept, 0.5, 0.0)
        gated = (jnp.tanh(mix[:hidden]) + 1.0) * (mix[hidden:] * mask)
        planes[pl.ds(i, hidden, stride=rows), :] = gated
        return carry

    lax.fori_loop(0, rows, body, 0, unroll=2)
    out[...] = planes[...].reshape(hidden, rows, cols).astype(jnp.bfloat16)


def project(pair, lengths, gain, bias, gate_w, value_w, row_blocks, slot_size, where=place):
    rows, cols, width = pair.shape
    hidden = gate_w.shape[1]
    whole = pl.BlockSpec((width, hidden), lambda b: (0, 0))
    vec = pl.BlockSpec((1, width), lambda b: (0, 0))
    return pl.pallas_call(
        functools.partial(project_kernel, rows, slot_size, where),
        grid=(row_blocks,),
        in_specs=[
            pl.BlockSpec(memory_space=pltpu.SMEM),
            pl.BlockSpec((PAD, cols, width), lambda b: (b, 0, 0)),
            vec,
            vec,
            whole,
            whole,
        ],
        out_specs=pl.BlockSpec((hidden, PAD, cols), lambda b: (0, b, 0)),
        out_shape=jax.ShapeDtypeStruct((hidden, PAD * row_blocks, cols), jnp.bfloat16),
        scratch_shapes=[
            pltpu.VMEM((2 * hidden, width), jnp.bfloat16),
            pltpu.VMEM((hidden * PAD, cols), jnp.float32),
        ],
        compiler_params=pltpu.CompilerParams(vmem_limit_bytes=32 << 20),
    )(lengths, pair, gain, bias, gate_w, value_w)


def product_kernel(left, right, out, left_mat, right_mat):
    groups, chans, rows, cols = left.shape
    blks = right.shape[0]
    for c in range(chans):
        span = pl.ds(c * cols, cols)
        left_mat[:, span] = left[:, c].reshape(groups * rows, cols)
        right_mat[:, span] = right[:, c].reshape(blks * PAD, cols)
    low = lax.broadcasted_iota(jnp.int32, (PAD, 2 * rows), 1) < rows
    pieces = 4
    part = blks // pieces
    for p in range(pieces):
        prod = dot(
            right_mat[p * part * PAD : (p + 1) * part * PAD],
            left_mat[...],
            (((1,), (1,)), ((), ())),
        )
        for q in range(part // 2):
            c = p * part // 2 + q
            for g in range(0, groups, 2):
                span = slice(g * rows, (g + 2) * rows)
                first = prod[2 * q * PAD : (2 * q + 1) * PAD, span]
                second = prod[(2 * q + 1) * PAD : (2 * q + 2) * PAD, span]
                out[g, c] = jnp.where(low, first, pltpu.roll(second, rows, 1)).astype(
                    jnp.bfloat16
                )
                out[g + 1, c] = jnp.where(low, pltpu.roll(first, rows, 1), second).astype(
                    jnp.bfloat16
                )


def product_of(left, right):
    groups, chans, rows, cols = left.shape
    blks = right.shape[0]
    return pl.pallas_call(
        product_kernel,
        out_shape=jax.ShapeDtypeStruct((groups, chans, PAD, 2 * rows), jnp.bfloat16),
        scratch_shapes=[
            pltpu.VMEM((groups * rows, chans * cols), jnp.bfloat16),
            pltpu.VMEM((blks * PAD, chans * cols), jnp.bfloat16),
        ],
        compiler_params=pltpu.CompilerParams(vmem_limit_bytes=48 << 20),
    )(left, right)


def update_kernel(
    out_gain,
    out_bias,
    slab,
    pair_a,
    pair_b,
    gain,
    bias,
    gate_w,
    out_w,
    out,
    normed_s,
    gate_s,
    out_s,
):
    hidden = slab.shape[0]
    rows, _, width = pair_a.shape
    for h, pair in enumerate((pair_a, pair_b)):
        flat = pair[...].reshape(rows * PAD, width).astype(jnp.float32)
        normed = normalize(flat, gain[...], bias[...]).astype(jnp.bfloat16)
        gate_s[h] = jax.nn.sigmoid(dot(normed, gate_w[...], (((1,), (0,)), ((), ()))))

    total = lax.fori_loop(
        0,
        hidden,
        lambda c, acc: acc + slab[c].astype(jnp.float32),
        jnp.zeros(slab.shape[1:], jnp.float32),
        unroll=8,
    )
    centre = total * (1.0 / hidden)

    def square(c, acc):
        centred = slab[c].astype(jnp.float32) - centre
        return acc + centred * centred

    squares = lax.fori_loop(0, hidden, square, jnp.zeros_like(centre), unroll=8)
    inv = lax.rsqrt(squares * (1.0 / hidden) + epsilon)

    def finish(c, carry):
        centred = slab[c].astype(jnp.float32) - centre
        normed_s[pl.ds(pl.multiple_of(c * PAD, PAD), PAD), :] = (
            centred * inv * out_gain[c] + out_bias[c]
        )
        return carry

    lax.fori_loop(0, hidden, finish, 0, unroll=8)
    span = 2 * PAD
    for r in range(JD):
        normed = normed_s[pl.ds(r, hidden, stride=PAD), :].astype(jnp.bfloat16)
        update = dot(normed, out_w[...], (((0,), (0,)), ((), ())))
        for h in range(2):
            gate = gate_s[h, pl.ds(r, rows, stride=PAD), :]
            out_s[pl.ds(h * JD + r, rows, stride=span), :] = (
                gate * update[h * rows : (h + 1) * rows]
            )
    whole = out_s[...].reshape(rows, span, width)
    out[...] = whole[:, : 2 * JD].astype(jnp.bfloat16)


def update_of(slab, pair, gain, bias, gate_w, out_gain, out_bias, out_w):
    rows, cols, width = pair.shape
    hidden = slab.shape[0]
    smem = pl.BlockSpec(memory_space=pltpu.SMEM)
    half = cols // 2 // PAD
    vec = pl.BlockSpec((1, width), lambda b: (0, 0))
    mat = pl.BlockSpec((width, width), lambda b: (0, 0))
    return pl.pallas_call(
        update_kernel,
        grid=(1,),
        in_specs=[
            smem,
            smem,
            pl.BlockSpec(slab.shape, lambda b: (0, 0, 0)),
            pl.BlockSpec((rows, PAD, width), lambda b: (0, 0, 0)),
            pl.BlockSpec((rows, PAD, width), lambda b: (0, half, 0)),
            vec,
            vec,
            mat,
            mat,
        ],
        out_specs=pl.BlockSpec((rows, 2 * JD, width), lambda b: (0, 0, 0)),
        out_shape=jax.ShapeDtypeStruct((rows, 2 * JD, width), jnp.bfloat16),
        scratch_shapes=[
            pltpu.VMEM((hidden * PAD, slab.shape[2]), jnp.float32),
            pltpu.VMEM((2, rows * PAD, width), jnp.float32),
            pltpu.VMEM((rows * 2 * PAD, width), jnp.float32),
        ],
        compiler_params=pltpu.CompilerParams(vmem_limit_bytes=32 << 20),
    )(out_gain, out_bias, slab, pair, pair, gain, bias, gate_w, out_w)


def on_device(
    pair_repr,
    chain_lengths,
    norm_gain,
    norm_bias,
    left_gate,
    left_value,
    right_gate,
    right_value,
    out_gain,
    out_bias,
    out_weight,
    gate_weight,
):
    rows, cols, width = pair_repr.shape
    groups = lax.axis_size("x") * lax.axis_size("core")
    chans = lax.axis_size("z") * lax.axis_size("yl")
    residues = rows * groups * lax.axis_size("yh")
    slot_size = residues // chain_lengths.shape[0]
    gain = norm_gain.reshape(1, width)
    bias = norm_bias.reshape(1, width)
    right = project(
        pair_repr, chain_lengths, gain, bias, right_gate, right_value, 1, slot_size
    )
    right = lax.all_to_all(right, SPREAD, 0, 0, tiled=True)
    pair_repr, right = lax.optimization_barrier((pair_repr, right))
    right = lax.all_gather(right, "yh", axis=0, tiled=True)
    left = project(
        pair_repr, chain_lengths, gain, bias, left_gate, left_value, rows // PAD, slot_size
    )
    left = lax.all_to_all(left, SPREAD, 0, 0, tiled=True)
    product = product_of(
        left.reshape(groups, chans, rows, cols), right.reshape(-1, chans, PAD, cols)
    )
    slab = lax.all_to_all(
        product.reshape(groups * chans, PAD, 2 * rows), SPREAD, 0, 0, tiled=True
    )
    return update_of(
        slab, pair_repr, gain, bias, gate_weight, out_gain, out_bias, out_weight
    )


def solution(mesh):
    names = tuple(name for name, _ in AXES)
    sizes = tuple(size for _, size in AXES)
    fine = Mesh(mesh.devices.reshape(sizes), names)
    split = P(names[:3], names[3:], None)
    return jax.shard_map(
        on_device,
        mesh=fine,
        in_specs=(split,) + (P(),) * 11,
        out_specs=split,
        check_vma=False,
    )
```

```python
import functools

import jax
import jax.numpy as jnp
from jax import lax
from jax.experimental import pallas as pl
from jax.experimental.pallas import tpu as pltpu
from jax.sharding import Mesh
from jax.sharding import PartitionSpec as P

JD = 13
PAD = 16
BATCH = 4
AXES = (("yh", 4), ("x", 4), ("core", 2), ("z", 8), ("yl", 2))
SPREAD = ("x", "core", "z", "yl")

epsilon = 1e-05

dot = functools.partial(lax.dot_general, preferred_element_type=jnp.float32)


def normalize(values, gain_vec, bias_vec):
    centre = jnp.mean(values, axis=-1, keepdims=True)
    centred = values - centre
    spread_sq = jnp.mean(centred * centred, axis=-1, keepdims=True)
    return centred * lax.rsqrt(spread_sq + epsilon) * gain_vec + bias_vec


def place():
    blk = (lax.axis_index("yh") * 4 + lax.axis_index("x")) * 2 + lax.axis_index("core")
    chan = lax.axis_index("z") * 2 + lax.axis_index("yl")
    return blk, chan


def real_left(lengths, start, slot_size):
    return lengths[start // slot_size] - start % slot_size


def prepare(gain, bias, gate_w, value_w, stack, scale, shift):
    width, hidden = gate_w.shape
    stack[:hidden] = (gate_w[...].astype(jnp.float32) * 0.5).T.astype(jnp.bfloat16)
    stack[hidden:] = value_w[...].astype(jnp.float32).T.astype(jnp.bfloat16)
    scale[...] = jnp.broadcast_to(gain[...], scale.shape).T
    shift[...] = jnp.broadcast_to(bias[...], shift.shape).T


def project_rows(pair, row_count, col_count, stack, scale, shift, planes, out):
    rows, cols, width = pair.shape
    hidden = stack.shape[0] // 2
    col_ids = lax.broadcasted_iota(jnp.int32, (1, cols), 1)
    scale_all = jnp.concatenate([scale[...]] * BATCH, axis=1)
    shift_all = jnp.concatenate([shift[...]] * BATCH, axis=1)
    for start in range(0, rows, BATCH):
        flat = pair[start : start + BATCH].reshape(BATCH * cols, width)
        values = flat.T.astype(jnp.float32)
        centre = jnp.mean(values, axis=0, keepdims=True)
        centred = values - centre
        spread_sq = jnp.mean(centred * centred, axis=0, keepdims=True)
        normed = centred * lax.rsqrt(spread_sq + epsilon) * scale_all + shift_all
        mix = dot(stack[...], normed.astype(jnp.bfloat16), (((1,), (0,)), ((), ())))
        gated = (jnp.tanh(mix[:hidden]) + 1.0) * mix[hidden:]
        for j in range(BATCH):
            i = start + j
            kept = jnp.where(i < row_count, col_count, 0)
            mask = jnp.where(col_ids < kept, 0.5, 0.0)
            planes[pl.ds(i, hidden, stride=rows), :] = gated[:, j * cols : (j + 1) * cols] * mask
    out[...] = planes[...].reshape(hidden, rows, cols).astype(jnp.bfloat16)


def in_hbm(*arrays):
    return [pltpu.with_memory_space_constraint(array, pltpu.HBM) for array in arrays]


def fetch(sems, *copies):
    started = [pltpu.make_async_copy(a, b, sems.at[n]) for n, (a, b) in enumerate(copies)]
    for copy in started:
        copy.start()
    return started


def right_kernel(
    limit,
    slot_size,
    where,
    lengths_h,
    pair_h,
    gain_h,
    bias_h,
    gate_h,
    value_h,
    out,
    lengths,
    pair,
    gain,
    bias,
    gate_w,
    value_w,
    stack,
    scale,
    shift,
    planes,
    sems,
):
    copies = fetch(
        sems,
        (gate_h, gate_w),
        (value_h, value_w),
        (gain_h, gain),
        (bias_h, bias),
        (lengths_h, lengths),
        (pair_h.at[pl.ds(0, PAD)], pair),
    )
    for copy in copies:
        copy.wait()
    blk, chan = where()
    prepare(gain, bias, gate_w, value_w, stack, scale, shift)
    row_count = real_left(lengths, blk * limit, slot_size)
    col_count = real_left(lengths, chan * pair.shape[1], slot_size)
    project_rows(pair, row_count, col_count, stack, scale, shift, planes, out)


def shared_scratch(width, hidden, cols):
    return [
        pltpu.VMEM((2 * hidden, width), jnp.bfloat16),
        pltpu.VMEM((width, cols), jnp.float32),
        pltpu.VMEM((width, cols), jnp.float32),
        pltpu.VMEM((hidden * PAD, cols), jnp.float32),
    ]


def project_right(pair, lengths, gain, bias, gate_w, value_w, slot_size, where=place):
    rows, cols, width = pair.shape
    hidden = gate_w.shape[1]
    return pl.pallas_call(
        functools.partial(right_kernel, rows, slot_size, where),
        in_specs=[pl.BlockSpec(memory_space=pltpu.HBM)] * 6,
        out_specs=pl.BlockSpec((hidden, PAD, cols), lambda: (0, 0, 0)),
        out_shape=jax.ShapeDtypeStruct((hidden, PAD, cols), jnp.bfloat16),
        scratch_shapes=[
            pltpu.SMEM(lengths.shape, jnp.int32),
            pltpu.VMEM((PAD, cols, width), jnp.bfloat16),
            pltpu.VMEM((1, width), jnp.float32),
            pltpu.VMEM((1, width), jnp.float32),
            pltpu.VMEM((width, hidden), jnp.bfloat16),
            pltpu.VMEM((width, hidden), jnp.bfloat16),
            *shared_scratch(width, hidden, cols),
            pltpu.SemaphoreType.DMA((6,)),
        ],
        compiler_params=pltpu.CompilerParams(vmem_limit_bytes=32 << 20),
    )(*in_hbm(lengths, pair, gain, bias, gate_w, value_w))


def left_kernel(
    limit, slot_size, where, lengths, pair, gain, bias, gate_w, value_w, out, stack, scale, shift, planes
):
    step = pl.program_id(0)
    blk, chan = where()

    @pl.when(step == 0)
    def _():
        prepare(gain, bias, gate_w, value_w, stack, scale, shift)

    row_count = real_left(lengths, blk * limit, slot_size) - step * PAD
    col_count = real_left(lengths, chan * pair.shape[1], slot_size)
    project_rows(pair, row_count, col_count, stack, scale, shift, planes, out)


def project_left(pair, lengths, gain, bias, gate_w, value_w, slot_size, where=place):
    rows, cols, width = pair.shape
    hidden = gate_w.shape[1]
    whole = pl.BlockSpec((width, hidden), lambda b: (0, 0))
    vec = pl.BlockSpec((1, width), lambda b: (0, 0))
    return pl.pallas_call(
        functools.partial(left_kernel, rows, slot_size, where),
        grid=(rows // PAD,),
        in_specs=[
            pl.BlockSpec(memory_space=pltpu.SMEM),
            pl.BlockSpec((PAD, cols, width), lambda b: (b, 0, 0)),
            vec,
            vec,
            whole,
            whole,
        ],
        out_specs=pl.BlockSpec((hidden, PAD, cols), lambda b: (0, b, 0)),
        out_shape=pltpu.HBM((hidden, rows, cols), jnp.bfloat16),
        scratch_shapes=shared_scratch(width, hidden, cols),
        cost_estimate=pl.CostEstimate(
            flops=4 * rows * cols * width * hidden,
            bytes_accessed=4 * rows * cols * width,
            transcendentals=rows * cols * hidden,
        ),
        compiler_params=pltpu.CompilerParams(vmem_limit_bytes=32 << 20),
    )(lengths, pair, gain, bias, gate_w, value_w)


def product_kernel(ring, where, *refs):
    left_h, rights_h = refs[0], refs[1 : 1 + ring]
    out, left_mat, right_mat, acc, sems = refs[1 + ring :]
    groups, chans, rows, cols = left_h.shape
    me = where()
    copies = []
    for c in range(chans):
        span = pl.ds(c * cols, cols)
        pairs = [(left_h.at[:, c], left_mat.at[:, :, span])]
        pairs += [
            (right.at[:, c], right_mat.at[pl.ds(d * groups, groups), :, span])
            for d, right in enumerate(rights_h)
        ]
        copies.append(fetch(sems.at[c], *pairs))
    size = 4
    for first in range(0, chans, size):
        for c in range(first, first + size):
            for copy in copies[c]:
                copy.wait()
        span = slice(first * cols, (first + size) * cols)
        part = dot(
            right_mat[:, :, span].reshape(ring * groups * PAD, size * cols),
            left_mat[:, :, span].reshape(groups * rows, size * cols),
            (((1,), (1,)), ((), ())),
        )
        if first == 0:
            acc[...] = part
        else:
            acc[...] += part
    low = lax.broadcasted_iota(jnp.int32, (PAD, 2 * rows), 1) < rows
    half = groups // 2
    for d in range(ring):
        base = lax.rem(me + ring - d, ring) * half
        for q in range(half):
            top = (d * groups + 2 * q) * PAD
            for g in range(0, groups, 2):
                span = slice(g * rows, (g + 2) * rows)
                first = acc[top : top + PAD, span]
                second = acc[top + PAD : top + 2 * PAD, span]
                out[g, base + q] = jnp.where(low, first, pltpu.roll(second, rows, 1)).astype(
                    jnp.bfloat16
                )
                out[g + 1, base + q] = jnp.where(
                    low, pltpu.roll(first, rows, 1), second
                ).astype(jnp.bfloat16)


def product_of(left, rights, where=lambda: lax.axis_index("yh")):
    groups, chans, rows, cols = left.shape
    ring = len(rights)
    hbm = pl.BlockSpec(memory_space=pltpu.HBM)
    return pl.pallas_call(
        functools.partial(product_kernel, ring, where),
        in_specs=[hbm] * (1 + ring),
        out_shape=jax.ShapeDtypeStruct((groups, chans, PAD, 2 * rows), jnp.bfloat16),
        scratch_shapes=[
            pltpu.VMEM((groups, rows, chans * cols), jnp.bfloat16),
            pltpu.VMEM((ring * groups, PAD, chans * cols), jnp.bfloat16),
            pltpu.VMEM((ring * groups * PAD, groups * rows), jnp.float32),
            pltpu.SemaphoreType.DMA((chans, 1 + ring)),
        ],
        compiler_params=pltpu.CompilerParams(vmem_limit_bytes=48 << 20),
    )(*in_hbm(left, *rights))


def gate_kernel(pair_a, pair_b, gain, bias, gate_w, out, gate_s):
    rows, _, width = pair_a.shape
    for h, pair in enumerate((pair_a, pair_b)):
        flat = pair[...].reshape(rows * PAD, width).astype(jnp.float32)
        normed = normalize(flat, gain[...], bias[...]).astype(jnp.bfloat16)
        gate_s[h] = jax.nn.sigmoid(dot(normed, gate_w[...], (((1,), (0,)), ((), ()))))
        for r in range(JD):
            out[h * JD + r] = gate_s[h, pl.ds(r, rows, stride=PAD), :]


def gate_of(pair, gain, bias, gate_w):
    rows, cols, width = pair.shape
    half = cols // 2 // PAD
    vec = pl.BlockSpec((1, width), lambda b: (0, 0))
    mat = pl.BlockSpec((width, width), lambda b: (0, 0))
    return pl.pallas_call(
        gate_kernel,
        grid=(1,),
        in_specs=[
            pl.BlockSpec((rows, PAD, width), lambda b: (0, 0, 0)),
            pl.BlockSpec((rows, PAD, width), lambda b: (0, half, 0)),
            vec,
            vec,
            mat,
        ],
        out_specs=pl.BlockSpec((2 * JD, rows, width), lambda b: (0, 0, 0)),
        out_shape=jax.ShapeDtypeStruct((2 * JD, rows, width), jnp.float32),
        scratch_shapes=[pltpu.VMEM((2, rows * PAD, width), jnp.float32)],
        compiler_params=pltpu.CompilerParams(vmem_limit_bytes=32 << 20),
    )(pair, pair, gain, bias, gate_w)


def update_kernel(out_gain, out_bias, slab, gate, out_w, out, normed_s):
    hidden = slab.shape[0]
    rows = gate.shape[1]
    total = lax.fori_loop(
        0,
        hidden,
        lambda c, acc: acc + slab[c].astype(jnp.float32),
        jnp.zeros(slab.shape[1:], jnp.float32),
        unroll=16,
    )
    centre = total * (1.0 / hidden)

    def square(c, acc):
        centred = slab[c].astype(jnp.float32) - centre
        return acc + centred * centred

    squares = lax.fori_loop(0, hidden, square, jnp.zeros_like(centre), unroll=16)
    inv = lax.rsqrt(squares * (1.0 / hidden) + epsilon)

    def finish(c, carry):
        centred = slab[c].astype(jnp.float32) - centre
        normed_s[pl.ds(pl.multiple_of(c * PAD, PAD), PAD), :] = (
            centred * inv * out_gain[c] + out_bias[c]
        )
        return carry

    lax.fori_loop(0, hidden, finish, 0, unroll=16)
    for r in range(JD):
        normed = normed_s[pl.ds(r, hidden, stride=PAD), :].astype(jnp.bfloat16)
        update = dot(normed, out_w[...], (((0,), (0,)), ((), ())))
        for h in range(2):
            m = h * JD + r
            out[m] = (gate[m] * update[h * rows : (h + 1) * rows]).astype(jnp.bfloat16)


def update_of(slab, gate, out_gain, out_bias, out_w):
    hidden = slab.shape[0]
    smem = pl.BlockSpec(memory_space=pltpu.SMEM)
    vmem = pl.BlockSpec(memory_space=pltpu.VMEM)
    return pl.pallas_call(
        update_kernel,
        in_specs=[smem, smem, vmem, vmem, vmem],
        out_specs=vmem,
        out_shape=jax.ShapeDtypeStruct(gate.shape, jnp.bfloat16),
        scratch_shapes=[pltpu.VMEM((hidden * PAD, slab.shape[2]), jnp.float32)],
        compiler_params=pltpu.CompilerParams(vmem_limit_bytes=32 << 20),
    )(out_gain, out_bias, slab, gate, out_w)


def on_device(
    pair_repr,
    chain_lengths,
    norm_gain,
    norm_bias,
    left_gate,
    left_value,
    right_gate,
    right_value,
    out_gain,
    out_bias,
    out_weight,
    gate_weight,
):
    rows, cols, width = pair_repr.shape
    groups = lax.axis_size("x") * lax.axis_size("core")
    chans = lax.axis_size("z") * lax.axis_size("yl")
    residues = rows * groups * lax.axis_size("yh")
    slot_size = residues // chain_lengths.shape[0]
    gain = norm_gain.reshape(1, width)
    bias = norm_bias.reshape(1, width)
    right = project_right(
        pair_repr, chain_lengths, gain, bias, right_gate, right_value, slot_size
    )
    right = lax.all_to_all(right, SPREAD, 0, 0, tiled=True)
    left = project_left(
        pair_repr, chain_lengths, gain, bias, left_gate, left_value, slot_size
    )
    left = lax.all_to_all(left, SPREAD, 0, 0, tiled=True)
    ring = lax.axis_size("yh")
    rights = [right] + [
        lax.ppermute(right, "yh", [(n, (n + d) % ring) for n in range(ring)])
        for d in range(1, ring)
    ]
    gate = gate_of(pair_repr, gain, bias, gate_weight)
    product = product_of(
        left.reshape(groups, chans, rows, cols),
        [part.reshape(groups, chans, PAD, cols) for part in rights],
    )
    slab = lax.all_to_all(
        product.reshape(groups * chans, PAD, 2 * rows), SPREAD, 0, 0, tiled=True
    )
    update = update_of(slab, gate, out_gain, out_bias, out_weight)
    return jnp.transpose(update, (1, 0, 2))


def solution(mesh):
    names = tuple(name for name, _ in AXES)
    sizes = tuple(size for _, size in AXES)
    fine = Mesh(mesh.devices.reshape(sizes), names)
    split = P(names[:3], names[3:], None)
    return jax.shard_map(
        on_device,
        mesh=fine,
        in_specs=(split,) + (P(),) * 11,
        out_specs=split,
        check_vma=False,
    )
```

```python
import functools

import jax
import jax.numpy as jnp
from jax import lax
from jax.experimental import pallas as pl
from jax.experimental.pallas import tpu as pltpu
from jax.sharding import Mesh
from jax.sharding import PartitionSpec as P

JD = 13
PAD = 16
BATCH = 4
AXES = (("yh", 4), ("x", 4), ("core", 2), ("z", 8), ("yl", 2))
SPREAD = ("yh", "core", "z", "yl")
RING = "x"

epsilon = 1e-05

dot = functools.partial(lax.dot_general, preferred_element_type=jnp.float32)


def normalize(values, gain_vec, bias_vec):
    centre = jnp.mean(values, axis=-1, keepdims=True)
    centred = values - centre
    spread_sq = jnp.mean(centred * centred, axis=-1, keepdims=True)
    return centred * lax.rsqrt(spread_sq + epsilon) * gain_vec + bias_vec


def place():
    blk = (lax.axis_index("yh") * 4 + lax.axis_index("x")) * 2 + lax.axis_index("core")
    chan = lax.axis_index("z") * 2 + lax.axis_index("yl")
    return blk, chan


def real_left(lengths, start, slot_size):
    return lengths[start // slot_size] - start % slot_size


def prepare(gain, bias, gate_w, value_w, stack, scale, shift):
    width, hidden = gate_w.shape
    stack[:hidden] = (gate_w[...].astype(jnp.float32) * 0.5).T.astype(jnp.bfloat16)
    stack[hidden:] = value_w[...].astype(jnp.float32).T.astype(jnp.bfloat16)
    scale[...] = jnp.broadcast_to(gain[...], scale.shape).T
    shift[...] = jnp.broadcast_to(bias[...], shift.shape).T


def project_rows(pair, row_count, col_count, stack, scale, shift, planes, out):
    rows, cols, width = pair.shape
    hidden = stack.shape[0] // 2
    col_ids = lax.broadcasted_iota(jnp.int32, (1, cols), 1)
    scale_all = jnp.concatenate([scale[...]] * BATCH, axis=1)
    shift_all = jnp.concatenate([shift[...]] * BATCH, axis=1)
    for start in range(0, rows, BATCH):
        flat = pair[start : start + BATCH].reshape(BATCH * cols, width)
        values = flat.T.astype(jnp.float32)
        centre = jnp.mean(values, axis=0, keepdims=True)
        centred = values - centre
        spread_sq = jnp.mean(centred * centred, axis=0, keepdims=True)
        normed = centred * lax.rsqrt(spread_sq + epsilon) * scale_all + shift_all
        mix = dot(stack[...], normed.astype(jnp.bfloat16), (((1,), (0,)), ((), ())))
        gated = (jnp.tanh(mix[:hidden]) + 1.0) * mix[hidden:]
        for j in range(BATCH):
            i = start + j
            kept = jnp.where(i < row_count, col_count, 0)
            mask = jnp.where(col_ids < kept, 0.5, 0.0)
            planes[pl.ds(i, hidden, stride=rows), :] = gated[:, j * cols : (j + 1) * cols] * mask
    out[...] = planes[...].reshape(hidden, rows, cols).astype(jnp.bfloat16)


def in_hbm(*arrays):
    return [pltpu.with_memory_space_constraint(array, pltpu.HBM) for array in arrays]


def fetch(sems, *copies):
    started = [pltpu.make_async_copy(a, b, sems.at[n]) for n, (a, b) in enumerate(copies)]
    for copy in started:
        copy.start()
    return started


def right_kernel(
    limit,
    slot_size,
    where,
    lengths_h,
    pair_h,
    gain_h,
    bias_h,
    gate_h,
    value_h,
    out,
    lengths,
    pair,
    gain,
    bias,
    gate_w,
    value_w,
    stack,
    scale,
    shift,
    planes,
    sems,
):
    copies = fetch(
        sems,
        (gate_h, gate_w),
        (value_h, value_w),
        (gain_h, gain),
        (bias_h, bias),
        (lengths_h, lengths),
        (pair_h.at[pl.ds(0, PAD)], pair),
    )
    for copy in copies:
        copy.wait()
    blk, chan = where()
    prepare(gain, bias, gate_w, value_w, stack, scale, shift)
    row_count = real_left(lengths, blk * limit, slot_size)
    col_count = real_left(lengths, chan * pair.shape[1], slot_size)
    project_rows(pair, row_count, col_count, stack, scale, shift, planes, out)


def shared_scratch(width, hidden, cols):
    return [
        pltpu.VMEM((2 * hidden, width), jnp.bfloat16),
        pltpu.VMEM((width, cols), jnp.float32),
        pltpu.VMEM((width, cols), jnp.float32),
        pltpu.VMEM((hidden * PAD, cols), jnp.float32),
    ]


def project_right(pair, lengths, gain, bias, gate_w, value_w, slot_size, where=place):
    rows, cols, width = pair.shape
    hidden = gate_w.shape[1]
    return pl.pallas_call(
        functools.partial(right_kernel, rows, slot_size, where),
        in_specs=[pl.BlockSpec(memory_space=pltpu.HBM)] * 6,
        out_specs=pl.BlockSpec((hidden, PAD, cols), lambda: (0, 0, 0)),
        out_shape=jax.ShapeDtypeStruct((hidden, PAD, cols), jnp.bfloat16),
        scratch_shapes=[
            pltpu.SMEM(lengths.shape, jnp.int32),
            pltpu.VMEM((PAD, cols, width), jnp.bfloat16),
            pltpu.VMEM((1, width), jnp.float32),
            pltpu.VMEM((1, width), jnp.float32),
            pltpu.VMEM((width, hidden), jnp.bfloat16),
            pltpu.VMEM((width, hidden), jnp.bfloat16),
            *shared_scratch(width, hidden, cols),
            pltpu.SemaphoreType.DMA((6,)),
        ],
        compiler_params=pltpu.CompilerParams(vmem_limit_bytes=32 << 20),
    )(*in_hbm(lengths, pair, gain, bias, gate_w, value_w))


def left_kernel(
    limit, slot_size, where, lengths, pair, gain, bias, gate_w, value_w, out, stack, scale, shift, planes
):
    step = pl.program_id(0)
    blk, chan = where()

    @pl.when(step == 0)
    def _():
        prepare(gain, bias, gate_w, value_w, stack, scale, shift)

    row_count = real_left(lengths, blk * limit, slot_size) - step * PAD
    col_count = real_left(lengths, chan * pair.shape[1], slot_size)
    project_rows(pair, row_count, col_count, stack, scale, shift, planes, out)


def project_left(pair, lengths, gain, bias, gate_w, value_w, slot_size, where=place):
    rows, cols, width = pair.shape
    hidden = gate_w.shape[1]
    whole = pl.BlockSpec((width, hidden), lambda b: (0, 0))
    vec = pl.BlockSpec((1, width), lambda b: (0, 0))
    return pl.pallas_call(
        functools.partial(left_kernel, rows, slot_size, where),
        grid=(rows // PAD,),
        in_specs=[
            pl.BlockSpec(memory_space=pltpu.SMEM),
            pl.BlockSpec((PAD, cols, width), lambda b: (b, 0, 0)),
            vec,
            vec,
            whole,
            whole,
        ],
        out_specs=pl.BlockSpec((hidden, PAD, cols), lambda b: (0, b, 0)),
        out_shape=pltpu.HBM((hidden, rows, cols), jnp.bfloat16),
        scratch_shapes=shared_scratch(width, hidden, cols),
        cost_estimate=pl.CostEstimate(
            flops=4 * rows * cols * width * hidden,
            bytes_accessed=4 * rows * cols * width,
            transcendentals=rows * cols * hidden,
        ),
        compiler_params=pltpu.CompilerParams(vmem_limit_bytes=32 << 20),
    )(lengths, pair, gain, bias, gate_w, value_w)


def product_kernel(ring, where, *refs):
    left_h, rights_h = refs[0], refs[1 : 1 + ring]
    out, left_mat, right_mat, acc, sems = refs[1 + ring :]
    groups, chans, rows, cols = left_h.shape
    me = where()
    copies = []
    for c in range(chans):
        span = pl.ds(c * cols, cols)
        pairs = [(left_h.at[:, c], left_mat.at[:, :, span])]
        pairs += [
            (right.at[:, c], right_mat.at[pl.ds(d * groups, groups), :, span])
            for d, right in enumerate(rights_h)
        ]
        copies.append(fetch(sems.at[c], *pairs))
    size = 4
    for first in range(0, chans, size):
        for c in range(first, first + size):
            for copy in copies[c]:
                copy.wait()
        span = slice(first * cols, (first + size) * cols)
        part = dot(
            right_mat[:, :, span].reshape(ring * groups * PAD, size * cols),
            left_mat[:, :, span].reshape(groups * rows, size * cols),
            (((1,), (1,)), ((), ())),
        )
        if first == 0:
            acc[...] = part
        else:
            acc[...] += part
    low = lax.broadcasted_iota(jnp.int32, (PAD, 2 * rows), 1) < rows
    half = groups // 2
    for d in range(ring):
        member = lax.rem(me + ring - d, ring)
        for q in range(half):
            top = (d * groups + 2 * q) * PAD
            for g in range(0, groups, 2):
                span = slice(g * rows, (g + 2) * rows)
                first = acc[top : top + PAD, span]
                second = acc[top + PAD : top + 2 * PAD, span]
                out[g, q * ring + member] = jnp.where(low, first, pltpu.roll(second, rows, 1)).astype(
                    jnp.bfloat16
                )
                out[g + 1, q * ring + member] = jnp.where(
                    low, pltpu.roll(first, rows, 1), second
                ).astype(jnp.bfloat16)


def product_of(left, rights, where=lambda: lax.axis_index(RING)):
    groups, chans, rows, cols = left.shape
    ring = len(rights)
    hbm = pl.BlockSpec(memory_space=pltpu.HBM)
    return pl.pallas_call(
        functools.partial(product_kernel, ring, where),
        in_specs=[hbm] * (1 + ring),
        out_shape=jax.ShapeDtypeStruct((groups, chans, PAD, 2 * rows), jnp.bfloat16),
        scratch_shapes=[
            pltpu.VMEM((groups, rows, chans * cols), jnp.bfloat16),
            pltpu.VMEM((ring * groups, PAD, chans * cols), jnp.bfloat16),
            pltpu.VMEM((ring * groups * PAD, groups * rows), jnp.float32),
            pltpu.SemaphoreType.DMA((chans, 1 + ring)),
        ],
        compiler_params=pltpu.CompilerParams(vmem_limit_bytes=48 << 20),
    )(*in_hbm(left, *rights))


def gate_kernel(pair_a, pair_b, gain, bias, gate_w, out, gate_s):
    rows, _, width = pair_a.shape
    for h, pair in enumerate((pair_a, pair_b)):
        flat = pair[...].reshape(rows * PAD, width).astype(jnp.float32)
        normed = normalize(flat, gain[...], bias[...]).astype(jnp.bfloat16)
        gate_s[h] = jax.nn.sigmoid(dot(normed, gate_w[...], (((1,), (0,)), ((), ()))))
        for r in range(JD):
            out[h * JD + r] = gate_s[h, pl.ds(r, rows, stride=PAD), :]


def gate_of(pair, gain, bias, gate_w):
    rows, cols, width = pair.shape
    half = cols // 2 // PAD
    vec = pl.BlockSpec((1, width), lambda b: (0, 0))
    mat = pl.BlockSpec((width, width), lambda b: (0, 0))
    return pl.pallas_call(
        gate_kernel,
        grid=(1,),
        in_specs=[
            pl.BlockSpec((rows, PAD, width), lambda b: (0, 0, 0)),
            pl.BlockSpec((rows, PAD, width), lambda b: (0, half, 0)),
            vec,
            vec,
            mat,
        ],
        out_specs=pl.BlockSpec((2 * JD, rows, width), lambda b: (0, 0, 0)),
        out_shape=jax.ShapeDtypeStruct((2 * JD, rows, width), jnp.float32),
        scratch_shapes=[pltpu.VMEM((2, rows * PAD, width), jnp.float32)],
        compiler_params=pltpu.CompilerParams(vmem_limit_bytes=32 << 20),
    )(pair, pair, gain, bias, gate_w)


def update_kernel(out_gain, out_bias, slab, gate, out_w, out, normed_s):
    hidden = slab.shape[0]
    rows = gate.shape[1]
    total = lax.fori_loop(
        0,
        hidden,
        lambda c, acc: acc + slab[c].astype(jnp.float32),
        jnp.zeros(slab.shape[1:], jnp.float32),
        unroll=16,
    )
    centre = total * (1.0 / hidden)

    def square(c, acc):
        centred = slab[c].astype(jnp.float32) - centre
        return acc + centred * centred

    squares = lax.fori_loop(0, hidden, square, jnp.zeros_like(centre), unroll=16)
    inv = lax.rsqrt(squares * (1.0 / hidden) + epsilon)

    def finish(c, carry):
        centred = slab[c].astype(jnp.float32) - centre
        normed_s[pl.ds(pl.multiple_of(c * PAD, PAD), PAD), :] = (
            centred * inv * out_gain[c] + out_bias[c]
        )
        return carry

    lax.fori_loop(0, hidden, finish, 0, unroll=16)
    for r in range(JD):
        normed = normed_s[pl.ds(r, hidden, stride=PAD), :].astype(jnp.bfloat16)
        update = dot(normed, out_w[...], (((0,), (0,)), ((), ())))
        for h in range(2):
            m = h * JD + r
            out[m] = (gate[m] * update[h * rows : (h + 1) * rows]).astype(jnp.bfloat16)


def update_of(slab, gate, out_gain, out_bias, out_w):
    hidden = slab.shape[0]
    smem = pl.BlockSpec(memory_space=pltpu.SMEM)
    vmem = pl.BlockSpec(memory_space=pltpu.VMEM)
    return pl.pallas_call(
        update_kernel,
        in_specs=[smem, smem, vmem, vmem, vmem],
        out_specs=vmem,
        out_shape=jax.ShapeDtypeStruct(gate.shape, jnp.bfloat16),
        scratch_shapes=[pltpu.VMEM((hidden * PAD, slab.shape[2]), jnp.float32)],
        compiler_params=pltpu.CompilerParams(vmem_limit_bytes=32 << 20),
    )(out_gain, out_bias, slab, gate, out_w)


def on_device(
    pair_repr,
    chain_lengths,
    norm_gain,
    norm_bias,
    left_gate,
    left_value,
    right_gate,
    right_value,
    out_gain,
    out_bias,
    out_weight,
    gate_weight,
):
    rows, cols, width = pair_repr.shape
    groups = lax.axis_size("yh") * lax.axis_size("core")
    chans = lax.axis_size("z") * lax.axis_size("yl")
    ring = lax.axis_size(RING)
    residues = rows * groups * ring
    slot_size = residues // chain_lengths.shape[0]
    gain = norm_gain.reshape(1, width)
    bias = norm_bias.reshape(1, width)
    right = project_right(
        pair_repr, chain_lengths, gain, bias, right_gate, right_value, slot_size
    )
    right = lax.all_to_all(right, SPREAD, 0, 0, tiled=True)
    left = project_left(
        pair_repr, chain_lengths, gain, bias, left_gate, left_value, slot_size
    )
    left = lax.all_to_all(left, SPREAD, 0, 0, tiled=True)
    rights = [right] + [
        lax.ppermute(right, RING, [(n, (n + d) % ring) for n in range(ring)])
        for d in range(1, ring)
    ]
    gate = gate_of(pair_repr, gain, bias, gate_weight)
    product = product_of(
        left.reshape(groups, chans, rows, cols),
        [part.reshape(groups, chans, PAD, cols) for part in rights],
    )
    slab = lax.all_to_all(
        product.reshape(groups * chans, PAD, 2 * rows), SPREAD, 0, 0, tiled=True
    )
    update = update_of(slab, gate, out_gain, out_bias, out_weight)
    return jnp.transpose(update, (1, 0, 2))


def solution(mesh):
    names = tuple(name for name, _ in AXES)
    sizes = tuple(size for _, size in AXES)
    fine = Mesh(mesh.devices.reshape(sizes), names)
    split = P(names[:3], names[3:], None)
    return jax.shard_map(
        on_device,
        mesh=fine,
        in_specs=(split,) + (P(),) * 11,
        out_specs=split,
        check_vma=False,
    )
```

```python
import functools

import jax
import jax.numpy as jnp
from jax import lax
from jax.experimental import pallas as pl
from jax.experimental.pallas import tpu as pltpu
from jax.sharding import Mesh
from jax.sharding import PartitionSpec as P

JD = 13
PAD = 16
BATCH = 4
AXES = (("yh", 4), ("x", 4), ("core", 2), ("z", 8), ("yl", 2))
SPREAD = ("yh", "z", "yl")
RING = "x"

epsilon = 1e-05

dot = functools.partial(lax.dot_general, preferred_element_type=jnp.float32)


def normalize(values, gain_vec, bias_vec):
    centre = jnp.mean(values, axis=-1, keepdims=True)
    centred = values - centre
    spread_sq = jnp.mean(centred * centred, axis=-1, keepdims=True)
    return centred * lax.rsqrt(spread_sq + epsilon) * gain_vec + bias_vec


def place():
    blk = (lax.axis_index("yh") * 4 + lax.axis_index("x")) * 2 + lax.axis_index("core")
    chan = lax.axis_index("z") * 2 + lax.axis_index("yl")
    return blk, chan


def real_left(lengths, start, slot_size):
    return lengths[start // slot_size] - start % slot_size


def prepare(gain, bias, gate_w, value_w, stack, scale, shift):
    width, hidden = gate_w.shape
    stack[:hidden] = (gate_w[...].astype(jnp.float32) * 0.5).T.astype(jnp.bfloat16)
    stack[hidden:] = value_w[...].astype(jnp.float32).T.astype(jnp.bfloat16)
    scale[...] = jnp.broadcast_to(gain[...], scale.shape).T
    shift[...] = jnp.broadcast_to(bias[...], shift.shape).T


def project_rows(pair, row_count, col_count, stack, scale, shift, planes, out):
    rows, cols, width = pair.shape
    hidden = stack.shape[0] // 2
    col_ids = lax.broadcasted_iota(jnp.int32, (1, cols), 1)
    scale_all = jnp.concatenate([scale[...]] * BATCH, axis=1)
    shift_all = jnp.concatenate([shift[...]] * BATCH, axis=1)
    for start in range(0, rows, BATCH):
        flat = pair[start : start + BATCH].reshape(BATCH * cols, width)
        values = flat.T.astype(jnp.float32)
        centre = jnp.mean(values, axis=0, keepdims=True)
        centred = values - centre
        spread_sq = jnp.mean(centred * centred, axis=0, keepdims=True)
        normed = centred * lax.rsqrt(spread_sq + epsilon) * scale_all + shift_all
        mix = dot(stack[...], normed.astype(jnp.bfloat16), (((1,), (0,)), ((), ())))
        gated = (jnp.tanh(mix[:hidden]) + 1.0) * mix[hidden:]
        for j in range(BATCH):
            i = start + j
            kept = jnp.where(i < row_count, col_count, 0)
            mask = jnp.where(col_ids < kept, 0.5, 0.0)
            planes[pl.ds(i, hidden, stride=rows), :] = gated[:, j * cols : (j + 1) * cols] * mask
    out[...] = planes[...].reshape(hidden, rows, cols).astype(jnp.bfloat16)


def in_hbm(*arrays):
    return [pltpu.with_memory_space_constraint(array, pltpu.HBM) for array in arrays]


def fetch(sems, *copies):
    started = [pltpu.make_async_copy(a, b, sems.at[n]) for n, (a, b) in enumerate(copies)]
    for copy in started:
        copy.start()
    return started


def right_kernel(
    limit,
    slot_size,
    where,
    lengths_h,
    pair_h,
    gain_h,
    bias_h,
    gate_h,
    value_h,
    out,
    lengths,
    pair,
    gain,
    bias,
    gate_w,
    value_w,
    stack,
    scale,
    shift,
    planes,
    sems,
):
    copies = fetch(
        sems,
        (gate_h, gate_w),
        (value_h, value_w),
        (gain_h, gain),
        (bias_h, bias),
        (lengths_h, lengths),
        (pair_h.at[pl.ds(0, PAD)], pair),
    )
    for copy in copies:
        copy.wait()
    blk, chan = where()
    prepare(gain, bias, gate_w, value_w, stack, scale, shift)
    row_count = real_left(lengths, blk * limit, slot_size)
    col_count = real_left(lengths, chan * pair.shape[1], slot_size)
    project_rows(pair, row_count, col_count, stack, scale, shift, planes, out)


def shared_scratch(width, hidden, cols):
    return [
        pltpu.VMEM((2 * hidden, width), jnp.bfloat16),
        pltpu.VMEM((width, cols), jnp.float32),
        pltpu.VMEM((width, cols), jnp.float32),
        pltpu.VMEM((hidden * PAD, cols), jnp.float32),
    ]


def project_right(pair, lengths, gain, bias, gate_w, value_w, slot_size, where=place):
    rows, cols, width = pair.shape
    hidden = gate_w.shape[1]
    return pl.pallas_call(
        functools.partial(right_kernel, rows, slot_size, where),
        in_specs=[pl.BlockSpec(memory_space=pltpu.HBM)] * 6,
        out_specs=pl.BlockSpec((hidden, PAD, cols), lambda: (0, 0, 0)),
        out_shape=jax.ShapeDtypeStruct((hidden, PAD, cols), jnp.bfloat16),
        scratch_shapes=[
            pltpu.SMEM(lengths.shape, jnp.int32),
            pltpu.VMEM((PAD, cols, width), jnp.bfloat16),
            pltpu.VMEM((1, width), jnp.float32),
            pltpu.VMEM((1, width), jnp.float32),
            pltpu.VMEM((width, hidden), jnp.bfloat16),
            pltpu.VMEM((width, hidden), jnp.bfloat16),
            *shared_scratch(width, hidden, cols),
            pltpu.SemaphoreType.DMA((6,)),
        ],
        compiler_params=pltpu.CompilerParams(vmem_limit_bytes=32 << 20),
    )(*in_hbm(lengths, pair, gain, bias, gate_w, value_w))


def left_kernel(
    limit, slot_size, where, lengths, pair, gain, bias, gate_w, value_w, out, stack, scale, shift, planes
):
    step = pl.program_id(0)
    blk, chan = where()

    @pl.when(step == 0)
    def _():
        prepare(gain, bias, gate_w, value_w, stack, scale, shift)

    row_count = real_left(lengths, blk * limit, slot_size) - step * PAD
    col_count = real_left(lengths, chan * pair.shape[1], slot_size)
    project_rows(pair, row_count, col_count, stack, scale, shift, planes, out)


def project_left(pair, lengths, gain, bias, gate_w, value_w, slot_size, where=place):
    rows, cols, width = pair.shape
    hidden = gate_w.shape[1]
    whole = pl.BlockSpec((width, hidden), lambda b: (0, 0))
    vec = pl.BlockSpec((1, width), lambda b: (0, 0))
    return pl.pallas_call(
        functools.partial(left_kernel, rows, slot_size, where),
        grid=(rows // PAD,),
        in_specs=[
            pl.BlockSpec(memory_space=pltpu.SMEM),
            pl.BlockSpec((PAD, cols, width), lambda b: (b, 0, 0)),
            vec,
            vec,
            whole,
            whole,
        ],
        out_specs=pl.BlockSpec((hidden, PAD, cols), lambda b: (0, b, 0)),
        out_shape=pltpu.HBM((hidden, rows, cols), jnp.bfloat16),
        scratch_shapes=shared_scratch(width, hidden, cols),
        cost_estimate=pl.CostEstimate(
            flops=4 * rows * cols * width * hidden,
            bytes_accessed=4 * rows * cols * width,
            transcendentals=rows * cols * hidden,
        ),
        compiler_params=pltpu.CompilerParams(vmem_limit_bytes=32 << 20),
    )(lengths, pair, gain, bias, gate_w, value_w)


def product_kernel(ring, where, *refs):
    count = 1 + 2 * ring
    sources, out, acc, sems, held = refs[:count], *refs[count : count + 3], refs[count + 3 :]
    left = held[0]
    groups, chans, hidden, rows, cols = left.shape
    paired = [held[1 + part * ring + d] for d in range(ring) for part in range(2)]
    half = chans // 2
    waves = [
        fetch(
            sems.at[h],
            *[
                (a.at[:, pl.ds(h * half, half)], b.at[:, pl.ds(h * half, half)])
                for a, b in zip(sources, held)
            ],
        )
        for h in range(2)
    ]
    me, core = where()
    low = lax.broadcasted_iota(jnp.int32, (PAD, 2 * rows), 1) < rows
    wide = 2

    def side(parts, first, ch):
        pieces = []
        for c in range(first, first + wide):
            tiles = [part[:, c, ch] for part in parts]
            height = tiles[0].shape[0] * tiles[0].shape[1]
            pieces.append(jnp.concatenate([t.reshape(height, cols) for t in tiles], axis=0))
        return jnp.concatenate(pieces, axis=1)

    for h, wave in enumerate(waves):
        for copy in wave:
            copy.wait()
        for ch in range(hidden):
            total = None if h == 0 else acc[ch].reshape(-1, groups * rows)
            for first in range(h * half, (h + 1) * half, wide):
                piece = dot(
                    side(paired, first, ch), side([left], first, ch), (((1,), (1,)), ((), ()))
                )
                total = piece if total is None else total + piece
            acc[ch] = total.reshape(acc.shape[1:])
    for ch in range(hidden):
        for d in range(ring):
            member = lax.rem(me + ring - d, ring)
            for q in range(groups):
                upper = acc.at[ch, d, core, q]
                lower = acc.at[ch, d, 1 - core, q]
                for g in range(0, groups, 2):
                    span = pl.ds(g * rows, 2 * rows)
                    u, v = upper[:, span], lower[:, span]
                    spot = q * ring + member
                    out[g, spot, ch] = jnp.where(low, u, pltpu.roll(v, rows, 1)).astype(
                        jnp.bfloat16
                    )
                    out[g + 1, spot, ch] = jnp.where(low, pltpu.roll(u, rows, 1), v).astype(
                        jnp.bfloat16
                    )


def product_of(left, own, other, where=lambda: (lax.axis_index(RING), lax.axis_index("core"))):
    groups, chans, hidden, rows, cols = left.shape
    ring = len(own)
    arrays = (left, *own, *other)
    return pl.pallas_call(
        functools.partial(product_kernel, ring, where),
        in_specs=[pl.BlockSpec(memory_space=pltpu.HBM)] * len(arrays),
        out_specs=pl.BlockSpec(memory_space=pltpu.VMEM),
        out_shape=jax.ShapeDtypeStruct((groups, chans, hidden, PAD, 2 * rows), jnp.bfloat16),
        scratch_shapes=[
            pltpu.VMEM((hidden, ring, 2, groups, PAD, groups * rows), jnp.float32),
            pltpu.SemaphoreType.DMA((2, len(arrays))),
            *[pltpu.VMEM(array.shape, jnp.bfloat16) for array in arrays],
        ],
        compiler_params=pltpu.CompilerParams(vmem_limit_bytes=48 << 20),
    )(*in_hbm(*arrays))


def gate_kernel(pair_a, pair_b, gain, bias, gate_w, out, gate_s):
    rows, _, width = pair_a.shape
    for h, pair in enumerate((pair_a, pair_b)):
        flat = pair[...].reshape(rows * PAD, width).astype(jnp.float32)
        normed = normalize(flat, gain[...], bias[...]).astype(jnp.bfloat16)
        gate_s[h] = jax.nn.sigmoid(dot(normed, gate_w[...], (((1,), (0,)), ((), ()))))
        for r in range(JD):
            out[h * JD + r] = gate_s[h, pl.ds(r, rows, stride=PAD), :]


def gate_of(pair, gain, bias, gate_w):
    rows, cols, width = pair.shape
    half = cols // 2 // PAD
    vec = pl.BlockSpec((1, width), lambda b: (0, 0))
    mat = pl.BlockSpec((width, width), lambda b: (0, 0))
    return pl.pallas_call(
        gate_kernel,
        grid=(1,),
        in_specs=[
            pl.BlockSpec((rows, PAD, width), lambda b: (0, 0, 0)),
            pl.BlockSpec((rows, PAD, width), lambda b: (0, half, 0)),
            vec,
            vec,
            mat,
        ],
        out_specs=pl.BlockSpec((2 * JD, rows, width), lambda b: (0, 0, 0)),
        out_shape=jax.ShapeDtypeStruct((2 * JD, rows, width), jnp.float32),
        scratch_shapes=[pltpu.VMEM((2, rows * PAD, width), jnp.float32)],
        compiler_params=pltpu.CompilerParams(vmem_limit_bytes=32 << 20),
    )(pair, pair, gain, bias, gate_w)


def update_kernel(out_gain, out_bias, slab, gate, out_w, out, normed_s):
    hidden = slab.shape[0]
    rows = gate.shape[1]
    total = lax.fori_loop(
        0,
        hidden,
        lambda c, acc: acc + slab[c].astype(jnp.float32),
        jnp.zeros(slab.shape[1:], jnp.float32),
        unroll=16,
    )
    centre = total * (1.0 / hidden)

    def square(c, acc):
        centred = slab[c].astype(jnp.float32) - centre
        return acc + centred * centred

    squares = lax.fori_loop(0, hidden, square, jnp.zeros_like(centre), unroll=16)
    inv = lax.rsqrt(squares * (1.0 / hidden) + epsilon)

    def finish(c, carry):
        centred = slab[c].astype(jnp.float32) - centre
        normed_s[pl.ds(pl.multiple_of(c * PAD, PAD), PAD), :] = (
            centred * inv * out_gain[c] + out_bias[c]
        )
        return carry

    lax.fori_loop(0, hidden, finish, 0, unroll=16)
    for r in range(JD):
        normed = normed_s[pl.ds(r, hidden, stride=PAD), :].astype(jnp.bfloat16)
        update = dot(normed, out_w[...], (((0,), (0,)), ((), ())))
        for h in range(2):
            m = h * JD + r
            out[m] = (gate[m] * update[h * rows : (h + 1) * rows]).astype(jnp.bfloat16)


def update_of(slab, gate, out_gain, out_bias, out_w):
    hidden = slab.shape[0]
    smem = pl.BlockSpec(memory_space=pltpu.SMEM)
    vmem = pl.BlockSpec(memory_space=pltpu.VMEM)
    return pl.pallas_call(
        update_kernel,
        in_specs=[smem, smem, vmem, vmem, vmem],
        out_specs=vmem,
        out_shape=jax.ShapeDtypeStruct(gate.shape, jnp.bfloat16),
        scratch_shapes=[pltpu.VMEM((hidden * PAD, slab.shape[2]), jnp.float32)],
        compiler_params=pltpu.CompilerParams(vmem_limit_bytes=32 << 20),
    )(out_gain, out_bias, slab, gate, out_w)


def on_device(
    pair_repr,
    chain_lengths,
    norm_gain,
    norm_bias,
    left_gate,
    left_value,
    right_gate,
    right_value,
    out_gain,
    out_bias,
    out_weight,
    gate_weight,
):
    rows, cols, width = pair_repr.shape
    hidden = left_gate.shape[1]
    groups = lax.axis_size("yh")
    chans = lax.axis_size("z") * lax.axis_size("yl")
    ring = lax.axis_size(RING)
    residues = rows * groups * ring * lax.axis_size("core")
    slot_size = residues // chain_lengths.shape[0]
    gain = norm_gain.reshape(1, width)
    bias = norm_bias.reshape(1, width)
    right = project_right(
        pair_repr, chain_lengths, gain, bias, right_gate, right_value, slot_size
    )
    right = lax.all_to_all(right, SPREAD, 0, 0, tiled=True)
    left = project_left(
        pair_repr, chain_lengths, gain, bias, left_gate, left_value, slot_size
    )
    left = lax.all_to_all(left, SPREAD, 0, 0, tiled=True)
    own = [right] + [
        lax.ppermute(right, RING, [(n, (n + d) % ring) for n in range(ring)])
        for d in range(1, ring)
    ]
    other = [lax.ppermute(part, "core", [(0, 1), (1, 0)]) for part in own]
    gate = gate_of(pair_repr, gain, bias, gate_weight)
    shape = (groups, chans, hidden // (groups * chans))
    product = product_of(
        left.reshape(*shape, rows, cols),
        [part.reshape(*shape, PAD, cols) for part in own],
        [part.reshape(*shape, PAD, cols) for part in other],
    )
    slab = lax.all_to_all(
        product.reshape(hidden, PAD, 2 * rows), SPREAD, 0, 0, tiled=True
    )
    update = update_of(slab, gate, out_gain, out_bias, out_weight)
    return jnp.transpose(update, (1, 0, 2))


def solution(mesh):
    names = tuple(name for name, _ in AXES)
    sizes = tuple(size for _, size in AXES)
    fine = Mesh(mesh.devices.reshape(sizes), names)
    split = P(names[:3], names[3:], None)
    return jax.shard_map(
        on_device,
        mesh=fine,
        in_specs=(split,) + (P(),) * 11,
        out_specs=split,
        check_vma=False,
    )
```

```python
import functools

import jax
import jax.numpy as jnp
from jax import lax
from jax.experimental import pallas as pl
from jax.experimental.pallas import tpu as pltpu
from jax.sharding import Mesh
from jax.sharding import PartitionSpec as P

JD = 13
PAD = 16
BATCH = 4
AXES = (("yh", 4), ("x", 4), ("core", 2), ("z", 8), ("yl", 2))
SPREAD = ("yl", "z", "yh")
RING = "x"

epsilon = 1e-05

dot = functools.partial(lax.dot_general, preferred_element_type=jnp.float32)


def normalize(values, gain_vec, bias_vec):
    centre = jnp.mean(values, axis=-1, keepdims=True)
    centred = values - centre
    spread_sq = jnp.mean(centred * centred, axis=-1, keepdims=True)
    return centred * lax.rsqrt(spread_sq + epsilon) * gain_vec + bias_vec


def place():
    blk = (lax.axis_index("yh") * 4 + lax.axis_index("x")) * 2 + lax.axis_index("core")
    chan = lax.axis_index("z") * 2 + lax.axis_index("yl")
    return blk, chan


def real_left(lengths, start, slot_size):
    return lengths[start // slot_size] - start % slot_size


def prepare(gain, bias, gate_w, value_w, stack, scale, shift):
    width, hidden = gate_w.shape
    stack[:hidden] = (gate_w[...].astype(jnp.float32) * 0.5).T.astype(jnp.bfloat16)
    stack[hidden:] = value_w[...].astype(jnp.float32).T.astype(jnp.bfloat16)
    scale[...] = jnp.broadcast_to(gain[...], scale.shape).T
    shift[...] = jnp.broadcast_to(bias[...], shift.shape).T


def project_rows(pair, row_count, col_count, stack, scale, shift, planes, out):
    rows, cols, width = pair.shape
    hidden = stack.shape[0] // 2
    col_ids = lax.broadcasted_iota(jnp.int32, (1, cols), 1)
    scale_all = jnp.concatenate([scale[...]] * BATCH, axis=1)
    shift_all = jnp.concatenate([shift[...]] * BATCH, axis=1)
    for start in range(0, rows, BATCH):
        flat = pair[start : start + BATCH].reshape(BATCH * cols, width)
        values = flat.T.astype(jnp.float32)
        centre = jnp.mean(values, axis=0, keepdims=True)
        centred = values - centre
        spread_sq = jnp.mean(centred * centred, axis=0, keepdims=True)
        normed = centred * lax.rsqrt(spread_sq + epsilon) * scale_all + shift_all
        mix = dot(stack[...], normed.astype(jnp.bfloat16), (((1,), (0,)), ((), ())))
        gated = (jnp.tanh(mix[:hidden]) + 1.0) * mix[hidden:]
        for j in range(BATCH):
            i = start + j
            kept = jnp.where(i < row_count, col_count, 0)
            mask = jnp.where(col_ids < kept, 0.5, 0.0)
            planes[pl.ds(i, hidden, stride=rows), :] = gated[:, j * cols : (j + 1) * cols] * mask
    out[...] = planes[...].reshape(hidden, rows, cols).astype(jnp.bfloat16)


def in_hbm(*arrays):
    return [pltpu.with_memory_space_constraint(array, pltpu.HBM) for array in arrays]


def fetch(sems, *copies):
    started = [pltpu.make_async_copy(a, b, sems.at[n]) for n, (a, b) in enumerate(copies)]
    for copy in started:
        copy.start()
    return started


def right_kernel(
    limit,
    slot_size,
    where,
    lengths_h,
    pair_h,
    gain_h,
    bias_h,
    gate_h,
    value_h,
    out,
    lengths,
    pair,
    gain,
    bias,
    gate_w,
    value_w,
    stack,
    scale,
    shift,
    planes,
    sems,
):
    copies = fetch(
        sems,
        (gate_h, gate_w),
        (value_h, value_w),
        (gain_h, gain),
        (bias_h, bias),
        (lengths_h, lengths),
        (pair_h.at[pl.ds(0, PAD)], pair),
    )
    for copy in copies:
        copy.wait()
    blk, chan = where()
    prepare(gain, bias, gate_w, value_w, stack, scale, shift)
    row_count = real_left(lengths, blk * limit, slot_size)
    col_count = real_left(lengths, chan * pair.shape[1], slot_size)
    project_rows(pair, row_count, col_count, stack, scale, shift, planes, out)


def shared_scratch(width, hidden, cols):
    return [
        pltpu.VMEM((2 * hidden, width), jnp.bfloat16),
        pltpu.VMEM((width, cols), jnp.float32),
        pltpu.VMEM((width, cols), jnp.float32),
        pltpu.VMEM((hidden * PAD, cols), jnp.float32),
    ]


def project_right(pair, lengths, gain, bias, gate_w, value_w, slot_size, where=place):
    rows, cols, width = pair.shape
    hidden = gate_w.shape[1]
    return pl.pallas_call(
        functools.partial(right_kernel, rows, slot_size, where),
        in_specs=[pl.BlockSpec(memory_space=pltpu.HBM)] * 6,
        out_specs=pl.BlockSpec((hidden, PAD, cols), lambda: (0, 0, 0)),
        out_shape=jax.ShapeDtypeStruct((hidden, PAD, cols), jnp.bfloat16),
        scratch_shapes=[
            pltpu.SMEM(lengths.shape, jnp.int32),
            pltpu.VMEM((PAD, cols, width), jnp.bfloat16),
            pltpu.VMEM((1, width), jnp.float32),
            pltpu.VMEM((1, width), jnp.float32),
            pltpu.VMEM((width, hidden), jnp.bfloat16),
            pltpu.VMEM((width, hidden), jnp.bfloat16),
            *shared_scratch(width, hidden, cols),
            pltpu.SemaphoreType.DMA((6,)),
        ],
        compiler_params=pltpu.CompilerParams(vmem_limit_bytes=32 << 20),
    )(*in_hbm(lengths, pair, gain, bias, gate_w, value_w))


def left_kernel(
    limit, slot_size, where, lengths, pair, gain, bias, gate_w, value_w, out, stack, scale, shift, planes
):
    step = pl.program_id(0)
    blk, chan = where()

    @pl.when(step == 0)
    def _():
        prepare(gain, bias, gate_w, value_w, stack, scale, shift)

    row_count = real_left(lengths, blk * limit, slot_size) - step * PAD
    col_count = real_left(lengths, chan * pair.shape[1], slot_size)
    project_rows(pair, row_count, col_count, stack, scale, shift, planes, out)


def project_left(pair, lengths, gain, bias, gate_w, value_w, slot_size, where=place):
    rows, cols, width = pair.shape
    hidden = gate_w.shape[1]
    whole = pl.BlockSpec((width, hidden), lambda b: (0, 0))
    vec = pl.BlockSpec((1, width), lambda b: (0, 0))
    return pl.pallas_call(
        functools.partial(left_kernel, rows, slot_size, where),
        grid=(rows // PAD,),
        in_specs=[
            pl.BlockSpec(memory_space=pltpu.SMEM),
            pl.BlockSpec((PAD, cols, width), lambda b: (b, 0, 0)),
            vec,
            vec,
            whole,
            whole,
        ],
        out_specs=pl.BlockSpec((hidden, PAD, cols), lambda b: (0, b, 0)),
        out_shape=pltpu.HBM((hidden, rows, cols), jnp.bfloat16),
        scratch_shapes=shared_scratch(width, hidden, cols),
        cost_estimate=pl.CostEstimate(
            flops=4 * rows * cols * width * hidden,
            bytes_accessed=4 * rows * cols * width,
            transcendentals=rows * cols * hidden,
        ),
        compiler_params=pltpu.CompilerParams(vmem_limit_bytes=32 << 20),
    )(lengths, pair, gain, bias, gate_w, value_w)


def product_kernel(ring, where, *refs):
    count = 1 + 2 * ring
    sources, out, acc, sems, held = refs[:count], *refs[count : count + 3], refs[count + 3 :]
    left = held[0]
    chans, groups, hidden, rows, cols = left.shape
    paired = [held[1 + part * ring + d] for d in range(ring) for part in range(2)]
    half = chans // 2
    waves = [
        fetch(
            sems.at[h],
            *[
                (a.at[pl.ds(h * half, half)], b.at[pl.ds(h * half, half)])
                for a, b in zip(sources, held)
            ],
        )
        for h in range(2)
    ]
    me, core, split = where()
    low = lax.broadcasted_iota(jnp.int32, (PAD, 2 * rows), 1) < rows
    wide = 2

    def side(parts, first, ch):
        pieces = []
        for c in range(first, first + wide):
            tiles = [part[c, :, ch] for part in parts]
            height = tiles[0].shape[0] * tiles[0].shape[1]
            pieces.append(jnp.concatenate([t.reshape(height, cols) for t in tiles], axis=0))
        return jnp.concatenate(pieces, axis=1)

    for h, wave in enumerate(waves):
        for copy in wave:
            copy.wait()
        for ch in range(hidden):
            total = None if h == 0 else acc[ch].reshape(-1, groups * rows)
            for first in range(h * half, (h + 1) * half, wide):
                piece = dot(
                    side(paired, first, ch), side([left], first, ch), (((1,), (1,)), ((), ()))
                )
                total = piece if total is None else total + piece
            acc[ch] = total.reshape(acc.shape[1:])
    for ch in range(hidden):
        for d in range(ring):
            member = lax.rem(me + ring - d, ring)
            for q in range(groups):
                piece = q * ring + member
                spot = lax.rem(piece, split) * (chans // split) + piece // split
                upper = acc.at[ch, d, core, q]
                lower = acc.at[ch, d, 1 - core, q]
                for g in range(0, groups, 2):
                    span = pl.ds(g * rows, 2 * rows)
                    u, v = upper[:, span], lower[:, span]
                    out[spot, g, ch] = jnp.where(low, u, pltpu.roll(v, rows, 1)).astype(
                        jnp.bfloat16
                    )
                    out[spot, g + 1, ch] = jnp.where(low, pltpu.roll(u, rows, 1), v).astype(
                        jnp.bfloat16
                    )


def product_place():
    return lax.axis_index(RING), lax.axis_index("core"), lax.axis_size("yl")


def product_of(left, own, other, where=product_place):
    chans, groups, hidden, rows, cols = left.shape
    ring = len(own)
    arrays = (left, *own, *other)
    return pl.pallas_call(
        functools.partial(product_kernel, ring, where),
        in_specs=[pl.BlockSpec(memory_space=pltpu.HBM)] * len(arrays),
        out_specs=pl.BlockSpec(memory_space=pltpu.VMEM),
        out_shape=jax.ShapeDtypeStruct((chans, groups, hidden, PAD, 2 * rows), jnp.bfloat16),
        scratch_shapes=[
            pltpu.VMEM((hidden, ring, 2, groups, PAD, groups * rows), jnp.float32),
            pltpu.SemaphoreType.DMA((2, len(arrays))),
            *[pltpu.VMEM(array.shape, jnp.bfloat16) for array in arrays],
        ],
        compiler_params=pltpu.CompilerParams(vmem_limit_bytes=48 << 20),
    )(*in_hbm(*arrays))


def gate_kernel(pair_a, pair_b, gain, bias, gate_w, out, gate_s):
    rows, _, width = pair_a.shape
    for h, pair in enumerate((pair_a, pair_b)):
        flat = pair[...].reshape(rows * PAD, width).astype(jnp.float32)
        normed = normalize(flat, gain[...], bias[...]).astype(jnp.bfloat16)
        gate_s[h] = jax.nn.sigmoid(dot(normed, gate_w[...], (((1,), (0,)), ((), ()))))
        for r in range(JD):
            out[h * JD + r] = gate_s[h, pl.ds(r, rows, stride=PAD), :]


def gate_of(pair, gain, bias, gate_w):
    rows, cols, width = pair.shape
    half = cols // 2 // PAD
    vec = pl.BlockSpec((1, width), lambda b: (0, 0))
    mat = pl.BlockSpec((width, width), lambda b: (0, 0))
    return pl.pallas_call(
        gate_kernel,
        grid=(1,),
        in_specs=[
            pl.BlockSpec((rows, PAD, width), lambda b: (0, 0, 0)),
            pl.BlockSpec((rows, PAD, width), lambda b: (0, half, 0)),
            vec,
            vec,
            mat,
        ],
        out_specs=pl.BlockSpec((2 * JD, rows, width), lambda b: (0, 0, 0)),
        out_shape=jax.ShapeDtypeStruct((2 * JD, rows, width), jnp.float32),
        scratch_shapes=[pltpu.VMEM((2, rows * PAD, width), jnp.float32)],
        compiler_params=pltpu.CompilerParams(vmem_limit_bytes=32 << 20),
    )(pair, pair, gain, bias, gate_w)


def update_kernel(out_gain, out_bias, slab, gate, out_w, out, normed_s):
    hidden = slab.shape[0]
    rows = gate.shape[1]
    total = lax.fori_loop(
        0,
        hidden,
        lambda c, acc: acc + slab[c].astype(jnp.float32),
        jnp.zeros(slab.shape[1:], jnp.float32),
        unroll=16,
    )
    centre = total * (1.0 / hidden)

    def square(c, acc):
        centred = slab[c].astype(jnp.float32) - centre
        return acc + centred * centred

    squares = lax.fori_loop(0, hidden, square, jnp.zeros_like(centre), unroll=16)
    inv = lax.rsqrt(squares * (1.0 / hidden) + epsilon)

    def finish(c, carry):
        centred = slab[c].astype(jnp.float32) - centre
        normed_s[pl.ds(pl.multiple_of(c * PAD, PAD), PAD), :] = (
            centred * inv * out_gain[c] + out_bias[c]
        )
        return carry

    lax.fori_loop(0, hidden, finish, 0, unroll=16)
    for r in range(JD):
        normed = normed_s[pl.ds(r, hidden, stride=PAD), :].astype(jnp.bfloat16)
        update = dot(normed, out_w[...], (((0,), (0,)), ((), ())))
        for h in range(2):
            m = h * JD + r
            out[m] = (gate[m] * update[h * rows : (h + 1) * rows]).astype(jnp.bfloat16)


def update_of(slab, gate, out_gain, out_bias, out_w):
    hidden = slab.shape[0]
    smem = pl.BlockSpec(memory_space=pltpu.SMEM)
    vmem = pl.BlockSpec(memory_space=pltpu.VMEM)
    return pl.pallas_call(
        update_kernel,
        in_specs=[smem, smem, vmem, vmem, vmem],
        out_specs=vmem,
        out_shape=jax.ShapeDtypeStruct(gate.shape, jnp.bfloat16),
        scratch_shapes=[pltpu.VMEM((hidden * PAD, slab.shape[2]), jnp.float32)],
        compiler_params=pltpu.CompilerParams(vmem_limit_bytes=32 << 20),
    )(out_gain, out_bias, slab, gate, out_w)


def on_device(
    pair_repr,
    chain_lengths,
    norm_gain,
    norm_bias,
    left_gate,
    left_value,
    right_gate,
    right_value,
    out_gain,
    out_bias,
    out_weight,
    gate_weight,
):
    rows, cols, width = pair_repr.shape
    hidden = left_gate.shape[1]
    groups = lax.axis_size("yh")
    chans = lax.axis_size("z") * lax.axis_size("yl")
    ring = lax.axis_size(RING)
    residues = rows * groups * ring * lax.axis_size("core")
    slot_size = residues // chain_lengths.shape[0]
    gain = norm_gain.reshape(1, width)
    bias = norm_bias.reshape(1, width)
    right = project_right(
        pair_repr, chain_lengths, gain, bias, right_gate, right_value, slot_size
    )
    right = lax.all_to_all(right, SPREAD, 0, 0, tiled=True)
    left = project_left(
        pair_repr, chain_lengths, gain, bias, left_gate, left_value, slot_size
    )
    left = lax.all_to_all(left, SPREAD, 0, 0, tiled=True)
    own = [right] + [
        lax.ppermute(right, RING, [(n, (n + d) % ring) for n in range(ring)])
        for d in range(1, ring)
    ]
    other = [lax.ppermute(part, "core", [(0, 1), (1, 0)]) for part in own]
    gate = gate_of(pair_repr, gain, bias, gate_weight)
    gate, own[0] = lax.optimization_barrier((gate, own[0]))
    shape = (chans, groups, hidden // (groups * chans))
    product = product_of(
        left.reshape(*shape, rows, cols),
        [part.reshape(*shape, PAD, cols) for part in own],
        [part.reshape(*shape, PAD, cols) for part in other],
    )
    slab = lax.all_to_all(
        product.reshape(hidden, PAD, 2 * rows), SPREAD, 0, 0, tiled=True
    )
    update = update_of(slab, gate, out_gain, out_bias, out_weight)
    return jnp.transpose(update, (1, 0, 2))


def solution(mesh):
    names = tuple(name for name, _ in AXES)
    sizes = tuple(size for _, size in AXES)
    fine = Mesh(mesh.devices.reshape(sizes), names)
    split = P(names[:3], names[3:], None)
    return jax.shard_map(
        on_device,
        mesh=fine,
        in_specs=(split,) + (P(),) * 11,
        out_specs=split,
        check_vma=False,
    )
```

```python
import functools

import jax
import jax.numpy as jnp
from jax import lax
from jax.experimental import pallas as pl
from jax.experimental.pallas import tpu as pltpu
from jax.sharding import Mesh
from jax.sharding import PartitionSpec as P

JD = 13
PAD = 16
BATCH = 4
AXES = (("yh", 4), ("x", 4), ("core", 2), ("z", 8), ("yl", 2))
SPREAD = ("yl", "z", "yh")
RING = "x"

epsilon = 1e-05

dot = functools.partial(lax.dot_general, preferred_element_type=jnp.float32)


def normalize(values, gain_vec, bias_vec):
    centre = jnp.mean(values, axis=-1, keepdims=True)
    centred = values - centre
    spread_sq = jnp.mean(centred * centred, axis=-1, keepdims=True)
    return centred * lax.rsqrt(spread_sq + epsilon) * gain_vec + bias_vec


def place():
    blk = (lax.axis_index("yh") * 4 + lax.axis_index("x")) * 2 + lax.axis_index("core")
    chan = lax.axis_index("z") * 2 + lax.axis_index("yl")
    return blk, chan


def real_left(lengths, start, slot_size):
    return lengths[start // slot_size] - start % slot_size


def spread_rows(ref, per):
    count = ref.shape[0] // per
    return jnp.concatenate([ref[pl.ds(j, count, stride=per), :] for j in range(per)], axis=0)


def columns(vec, like):
    return jnp.broadcast_to(vec[...], like.shape).T


def prepare(gain, bias, gate_w, value_w, stack, scale, shift, per):
    hidden = gate_w.shape[1]
    scale[...] = (gate_w[...].astype(jnp.float32) * 0.5).T
    stack[:hidden] = spread_rows(scale, per).astype(jnp.bfloat16)
    scale[...] = value_w[...].astype(jnp.float32).T
    stack[hidden:] = spread_rows(scale, per).astype(jnp.bfloat16)
    scale[...] = columns(gain, scale)
    shift[...] = columns(bias, shift)


def project_rows(pair, row_count, col_count, stack, scale, shift, store):
    rows, cols, width = pair.shape
    hidden = stack.shape[0] // 2
    col_ids = lax.broadcasted_iota(jnp.int32, (1, cols), 1)
    for start in range(0, rows, BATCH):
        batch = min(BATCH, rows - start)
        flat = pair[start : start + batch].reshape(batch * cols, width)
        values = flat.T.astype(jnp.float32)
        centre = jnp.mean(values, axis=0, keepdims=True)
        centred = values - centre
        spread_sq = jnp.mean(centred * centred, axis=0, keepdims=True)
        scale_all = jnp.concatenate([scale[...]] * batch, axis=1)
        shift_all = jnp.concatenate([shift[...]] * batch, axis=1)
        normed = centred * lax.rsqrt(spread_sq + epsilon) * scale_all + shift_all
        mix = dot(stack[...], normed.astype(jnp.bfloat16), (((1,), (0,)), ((), ())))
        gated = (jnp.tanh(mix[:hidden]) + 1.0) * mix[hidden:]
        for j in range(batch):
            i = start + j
            kept = jnp.where(i < row_count, col_count, 0)
            mask = jnp.where(col_ids < kept, 0.5, 0.0)
            store(i, gated[:, j * cols : (j + 1) * cols] * mask)


def in_hbm(*arrays):
    return [pltpu.with_memory_space_constraint(array, pltpu.HBM) for array in arrays]


def fetch(sems, *copies):
    started = [pltpu.make_async_copy(a, b, sems.at[n]) for n, (a, b) in enumerate(copies)]
    for copy in started:
        copy.start()
    return started


def right_kernel(
    per,
    limit,
    slot_size,
    where,
    lengths_h,
    pair_h,
    gain_h,
    bias_h,
    gate_h,
    value_h,
    out,
    lengths,
    pair,
    gain,
    bias,
    gate_w,
    value_w,
    stack,
    scale,
    shift,
    planes,
    sems,
):
    copies = fetch(
        sems,
        (gate_h, gate_w),
        (value_h, value_w),
        (gain_h, gain),
        (bias_h, bias),
        (lengths_h, lengths),
        (pair_h.at[pl.ds(0, JD)], pair),
    )
    for copy in copies:
        copy.wait()
    blk, chan = where()
    prepare(gain, bias, gate_w, value_w, stack, scale, shift, per)
    row_count = real_left(lengths, blk * limit, slot_size)
    col_count = real_left(lengths, chan * pair.shape[1], slot_size)
    peers = stack.shape[0] // 2 // per

    def store(i, value):
        for j in range(per):
            planes[pl.ds(i * per + j, peers, stride=JD * per), :] = value[
                j * peers : (j + 1) * peers
            ]

    project_rows(pair, row_count, col_count, stack, scale, shift, store)
    out[...] = planes[...].astype(jnp.bfloat16)


def shared_scratch(width, hidden, cols, rows):
    return [
        pltpu.VMEM((2 * hidden, width), jnp.bfloat16),
        pltpu.VMEM((width, cols), jnp.float32),
        pltpu.VMEM((width, cols), jnp.float32),
        pltpu.VMEM((hidden * rows, cols), jnp.float32),
    ]


def project_right(pair, lengths, gain, bias, gate_w, value_w, slot_size, per, where=place):
    rows, cols, width = pair.shape
    hidden = gate_w.shape[1]
    return pl.pallas_call(
        functools.partial(right_kernel, per, rows, slot_size, where),
        in_specs=[pl.BlockSpec(memory_space=pltpu.HBM)] * 6,
        out_specs=pl.BlockSpec((hidden * JD, cols), lambda: (0, 0)),
        out_shape=jax.ShapeDtypeStruct((hidden * JD, cols), jnp.bfloat16),
        scratch_shapes=[
            pltpu.SMEM(lengths.shape, jnp.int32),
            pltpu.VMEM((JD, cols, width), jnp.bfloat16),
            pltpu.VMEM((1, width), jnp.float32),
            pltpu.VMEM((1, width), jnp.float32),
            pltpu.VMEM((width, hidden), jnp.bfloat16),
            pltpu.VMEM((width, hidden), jnp.bfloat16),
            *shared_scratch(width, hidden, cols, JD),
            pltpu.SemaphoreType.DMA((6,)),
        ],
        compiler_params=pltpu.CompilerParams(vmem_limit_bytes=32 << 20),
    )(*in_hbm(lengths, pair, gain, bias, gate_w, value_w))


def left_kernel(
    limit, slot_size, where, lengths, pair, gain, bias, gate_w, value_w, out, stack, scale, shift, planes
):
    step = pl.program_id(0)
    blk, chan = where()

    @pl.when(step == 0)
    def _():
        prepare(gain, bias, gate_w, value_w, stack, scale, shift, 1)

    row_count = real_left(lengths, blk * limit, slot_size) - step * PAD
    col_count = real_left(lengths, chan * pair.shape[1], slot_size)
    rows, cols, _ = pair.shape
    hidden = stack.shape[0] // 2

    def store(i, value):
        planes[pl.ds(i, hidden, stride=rows), :] = value

    project_rows(pair, row_count, col_count, stack, scale, shift, store)
    out[...] = planes[...].reshape(hidden, rows, cols).astype(jnp.bfloat16)


def project_left(pair, lengths, gain, bias, gate_w, value_w, slot_size, where=place):
    rows, cols, width = pair.shape
    hidden = gate_w.shape[1]
    whole = pl.BlockSpec((width, hidden), lambda b: (0, 0))
    vec = pl.BlockSpec((1, width), lambda b: (0, 0))
    return pl.pallas_call(
        functools.partial(left_kernel, rows, slot_size, where),
        grid=(rows // PAD,),
        in_specs=[
            pl.BlockSpec(memory_space=pltpu.SMEM),
            pl.BlockSpec((PAD, cols, width), lambda b: (b, 0, 0)),
            vec,
            vec,
            whole,
            whole,
        ],
        out_specs=pl.BlockSpec((hidden, PAD, cols), lambda b: (0, b, 0)),
        out_shape=pltpu.HBM((hidden, rows, cols), jnp.bfloat16),
        scratch_shapes=shared_scratch(width, hidden, cols, PAD),
        cost_estimate=pl.CostEstimate(
            flops=4 * rows * cols * width * hidden,
            bytes_accessed=4 * rows * cols * width,
            transcendentals=rows * cols * hidden,
        ),
        compiler_params=pltpu.CompilerParams(vmem_limit_bytes=32 << 20),
    )(lengths, pair, gain, bias, gate_w, value_w)


def product_kernel(ring, where, *refs):
    count = 1 + 2 * ring
    left_h, own, other = refs[0], refs[1 : 1 + ring], refs[1 + ring : count]
    out, left, right, acc, stage, sems = refs[count:]
    chans, groups, hidden, rows, cols = left.shape
    height = own[0].shape[1]
    seg = height // groups
    half = chans // 2
    paired = [part for two in zip(own, other) for part in two]
    waves = []
    for h in range(2):
        part = pl.ds(h * half, half)
        waves.append(
            fetch(
                sems.at[h],
                (left_h.at[part], left.at[part]),
                *[
                    (a.at[part], right.at[part, pl.ds(n * height, height)])
                    for n, a in enumerate(paired)
                ],
            )
        )
    me, core, split = where()
    wide = 4
    parity = lax.broadcasted_iota(jnp.int32, (right.shape[1], groups * rows), 0) % hidden
    for h, wave in enumerate(waves):
        for copy in wave:
            copy.wait()
        for first in range(h * half, (h + 1) * half, wide):
            block = range(first, first + wide)
            lhs = jnp.concatenate([right[c] for c in block], axis=1)
            piece = None
            for ch in range(hidden):
                rhs = jnp.concatenate(
                    [left[c, :, ch].reshape(groups * rows, cols) for c in block], axis=1
                )
                part = dot(lhs, rhs, (((1,), (1,)), ((), ())))
                piece = part if piece is None else jnp.where(parity == ch, part, piece)
            if first == 0:
                acc[...] = piece.reshape(acc.shape)
            else:
                acc[...] += piece.reshape(acc.shape)
    low = lax.broadcasted_iota(jnp.int32, (seg, 2 * rows), 1) < rows
    for d in range(ring):
        member = lax.rem(me + ring - d, ring)
        for q in range(groups):
            piece = q * ring + member
            spot = lax.rem(piece, split) * (chans // split) + piece // split
            band = pl.ds(q * seg, seg)
            for g in range(0, groups, 2):
                span = pl.ds(g * rows, 2 * rows)
                u = acc[2 * d + core, band, span]
                v = acc[2 * d + 1 - core, band, span]
                stage[spot, pl.ds(g * seg, seg), :] = jnp.where(low, u, pltpu.roll(v, rows, 1))
                stage[spot, pl.ds((g + 1) * seg, seg), :] = jnp.where(
                    low, pltpu.roll(u, rows, 1), v
                )
    out[...] = stage[...].astype(jnp.bfloat16)


def product_place():
    return lax.axis_index(RING), lax.axis_index("core"), lax.axis_size("yl")


def product_of(left, own, other, where=product_place):
    chans, groups, hidden, rows, cols = left.shape
    ring = len(own)
    height = own[0].shape[1]
    arrays = (left, *own, *other)
    return pl.pallas_call(
        functools.partial(product_kernel, ring, where),
        in_specs=[pl.BlockSpec(memory_space=pltpu.HBM)] * len(arrays),
        out_specs=pl.BlockSpec(memory_space=pltpu.VMEM),
        out_shape=jax.ShapeDtypeStruct((chans, height, 2 * rows), jnp.bfloat16),
        scratch_shapes=[
            pltpu.VMEM(left.shape, jnp.bfloat16),
            pltpu.VMEM((chans, 2 * ring * height, cols), jnp.bfloat16),
            pltpu.VMEM((2 * ring, height, groups * rows), jnp.float32),
            pltpu.VMEM((chans, height, 2 * rows), jnp.float32),
            pltpu.SemaphoreType.DMA((2, len(arrays))),
        ],
        compiler_params=pltpu.CompilerParams(vmem_limit_bytes=48 << 20),
    )(*in_hbm(*arrays))


def gate_kernel(
    per,
    pair_a,
    pair_b,
    gain,
    bias,
    gate_w,
    out_gain,
    out_bias,
    out_w,
    out,
    scale,
    shift,
    weight,
    gate_s,
    turn,
):
    rows, _, width = pair_a.shape
    for h, pair in enumerate((pair_a, pair_b)):
        flat = pair[...].reshape(rows * PAD, width).astype(jnp.float32)
        normed = normalize(flat, gain[...], bias[...]).astype(jnp.bfloat16)
        gate_s[h] = jax.nn.sigmoid(dot(normed, gate_w[...], (((1,), (0,)), ((), ()))))
        for r in range(JD):
            out[h * JD + r] = gate_s[h, pl.ds(r, rows, stride=PAD), :]
    turn[...] = columns(out_gain, turn)
    scale[...] = spread_rows(turn, per)
    turn[...] = columns(out_bias, turn)
    shift[...] = spread_rows(turn, per)
    turn[...] = out_w[...].astype(jnp.float32)
    weight[...] = spread_rows(turn, per).astype(jnp.bfloat16)


def gate_of(pair, gain, bias, gate_w, out_gain, out_bias, out_w, per):
    rows, cols, width = pair.shape
    half = cols // 2 // PAD
    vec = pl.BlockSpec((1, width), lambda b: (0, 0))
    mat = pl.BlockSpec((width, width), lambda b: (0, 0))
    return pl.pallas_call(
        functools.partial(gate_kernel, per),
        grid=(1,),
        in_specs=[
            pl.BlockSpec((rows, PAD, width), lambda b: (0, 0, 0)),
            pl.BlockSpec((rows, PAD, width), lambda b: (0, half, 0)),
            vec,
            vec,
            mat,
            vec,
            vec,
            mat,
        ],
        out_specs=[pl.BlockSpec((2 * JD, rows, width), lambda b: (0, 0, 0)), mat, mat, mat],
        out_shape=[
            jax.ShapeDtypeStruct((2 * JD, rows, width), jnp.float32),
            jax.ShapeDtypeStruct((width, width), jnp.float32),
            jax.ShapeDtypeStruct((width, width), jnp.float32),
            jax.ShapeDtypeStruct((width, width), jnp.bfloat16),
        ],
        scratch_shapes=[
            pltpu.VMEM((2, rows * PAD, width), jnp.float32),
            pltpu.VMEM((width, width), jnp.float32),
        ],
        compiler_params=pltpu.CompilerParams(vmem_limit_bytes=32 << 20),
    )(pair, pair, gain, bias, gate_w, out_gain, out_bias, out_w)


def update_kernel(per, slab, gate, scale, shift, weight, out, plain):
    hidden = weight.shape[0]
    rows = gate.shape[1]
    peers = hidden // per
    plain[...] = slab[...].astype(jnp.float32)
    for r in range(JD):
        values = jnp.concatenate(
            [plain[pl.ds(r * per + j, peers, stride=JD * per), :] for j in range(per)], axis=0
        )
        centre = jnp.mean(values, axis=0, keepdims=True)
        centred = values - centre
        spread_sq = jnp.mean(centred * centred, axis=0, keepdims=True)
        normed = centred * lax.rsqrt(spread_sq + epsilon) * scale[...] + shift[...]
        update = dot(normed.astype(jnp.bfloat16), weight[...], (((0,), (0,)), ((), ())))
        for h in range(2):
            m = h * JD + r
            out[m] = (gate[m] * update[h * rows : (h + 1) * rows]).astype(jnp.bfloat16)


def update_of(slab, gate, scale, shift, weight, per):
    vmem = pl.BlockSpec(memory_space=pltpu.VMEM)
    return pl.pallas_call(
        functools.partial(update_kernel, per),
        in_specs=[vmem] * 5,
        out_specs=vmem,
        out_shape=jax.ShapeDtypeStruct(gate.shape, jnp.bfloat16),
        scratch_shapes=[pltpu.VMEM(slab.shape, jnp.float32)],
        compiler_params=pltpu.CompilerParams(vmem_limit_bytes=32 << 20),
    )(slab, gate, scale, shift, weight)


def on_device(
    pair_repr,
    chain_lengths,
    norm_gain,
    norm_bias,
    left_gate,
    left_value,
    right_gate,
    right_value,
    out_gain,
    out_bias,
    out_weight,
    gate_weight,
):
    rows, cols, width = pair_repr.shape
    hidden = left_gate.shape[1]
    groups = lax.axis_size("yh")
    chans = lax.axis_size("z") * lax.axis_size("yl")
    ring = lax.axis_size(RING)
    residues = rows * groups * ring * lax.axis_size("core")
    slot_size = residues // chain_lengths.shape[0]
    gain = norm_gain.reshape(1, width)
    bias = norm_bias.reshape(1, width)
    peers = chans * groups
    per = hidden // peers
    message = (peers, JD, per, cols)
    right = project_right(
        pair_repr, chain_lengths, gain, bias, right_gate, right_value, slot_size, per
    )
    right = lax.all_to_all(right.reshape(message), SPREAD, 0, 0, tiled=True)
    left = project_left(
        pair_repr, chain_lengths, gain, bias, left_gate, left_value, slot_size
    )
    left = lax.all_to_all(left, SPREAD, 0, 0, tiled=True)
    own = [right] + [
        lax.ppermute(right, RING, [(n, (n + d) % ring) for n in range(ring)])
        for d in range(1, ring)
    ]
    other = [lax.ppermute(part, "core", [(0, 1), (1, 0)]) for part in own]
    gate, scale, shift, weight = gate_of(
        pair_repr,
        gain,
        bias,
        gate_weight,
        out_gain.reshape(1, hidden),
        out_bias.reshape(1, hidden),
        out_weight,
        per,
    )
    gate, own[0] = lax.optimization_barrier((gate, own[0]))
    band = (chans, groups * JD * per, cols)
    product = product_of(
        left.reshape(chans, groups, per, rows, cols),
        [part.reshape(band) for part in own],
        [part.reshape(band) for part in other],
    )
    slab = lax.all_to_all(
        product.reshape(peers, JD, per, 2 * rows), SPREAD, 0, 0, tiled=True
    )
    update = update_of(slab.reshape(hidden * JD, 2 * rows), gate, scale, shift, weight, per)
    return jnp.transpose(update, (1, 0, 2))


def solution(mesh):
    names = tuple(name for name, _ in AXES)
    sizes = tuple(size for _, size in AXES)
    fine = Mesh(mesh.devices.reshape(sizes), names)
    split = P(names[:3], names[3:], None)
    return jax.shard_map(
        on_device,
        mesh=fine,
        in_specs=(split,) + (P(),) * 11,
        out_specs=split,
        check_vma=False,
    )
```
